128 devices in a mesh: row: 8 (over z, core), col: 16 (over y, x).
Axes of the slice: x: 4, y: 4, z: 4, core: 2. Of those that a mesh axis runs over, the one named last changes fastest.
Arguments:
- left_amps: bfloat16 [8192, 8192], P('row', 'col'), may hold values from -6 to 6
- right_ints: bfloat16 [8192, 16384], P('row', 'col'), may hold values from -0.0625 to 0.0625
- left_mask: int32 [64, 64], P('row', 'col'), may hold values from 0 to 1, as said below
- right_mask: int32 [64, 128], P('row', 'col'), may hold values from 0 to 1, as said below
- result_mask: int32 [64, 128], P('row', 'col'), may hold values from 0 to 1, as said below
Outputs:
- pair_major: bfloat16 [128, 1048576], P(None, ('row', 'col'))
The draws below stay inside these ranges and needn't reach their ends.
Inputs may be any that keep to these rules, and one draw needn't show every extreme that they name: `left_mask`: a tile is kept (1) or left out (0). `right_mask`: a tile is kept (1) or left out (0). `result_mask`: a tile is kept (1) or left out (0).
All inputs are finite; a program needn't handle non-finite values.
Results may differ from the reference program's by a relative error of at most 0.001.
Values may be sent and summed in bfloat16 or wider, within the bound.
A program may use at most 128 MiB of HBM per device.

```python
import jax
import jax.numpy as jnp

TILE = 128
KW = 8192
ROWS_DEV = 1024
COLS_DEV = 1024
MROWS = 8192
NCOLS = 16384
N_ROW = 8
N_COL = 16


def band_mask(key, tile_rows, tile_cols):
    row_index = jnp.arange(tile_rows, dtype=jnp.int32)[:, None]
    col_index = jnp.arange(tile_cols, dtype=jnp.int32)[None, :]
    distance = jnp.abs(row_index * tile_cols - col_index * tile_rows)
    breadth = max(tile_rows * tile_cols * 3 // 10, 1)
    threshold = 250 + 650 * jnp.maximum(breadth - distance, 0) // breadth
    rolled = jax.random.randint(key, (tile_rows, tile_cols), 0, 1000, dtype=jnp.int32)
    return (rolled < threshold).astype(jnp.int32)


def draw_left_mask(key, part):
    return band_mask(jax.random.fold_in(key, 11), MROWS // TILE, KW // TILE)


def draw_right_mask(key, part):
    return band_mask(jax.random.fold_in(key, 23), KW // TILE, NCOLS // TILE)


def draw_result_mask(key, part):
    return band_mask(jax.random.fold_in(key, 37), MROWS // TILE, NCOLS // TILE)


def shard_levels(own_key, dims, split, low, top_value):
    def one(axis_at, shards_of):
        heights = jax.random.uniform(jax.random.fold_in(jax.random.fold_in(own_key, 6), axis_at), (shards_of,), jnp.float32, low / len(split), top_value / len(split))
        return jnp.repeat(jnp.exp(heights), dims[axis_at] // shards_of).reshape((-1,) + (1,) * (len(dims) - axis_at - 1))

    factor_of = one(*split[0])
    for cut in split[1:]:
        factor_of = factor_of * one(*cut)
    return factor_of


def normal_values(own_key, extent, width, reach, shards=(), held_as=jnp.bfloat16):
    result = width * jax.random.normal(own_key, extent, jnp.float32)
    if shards:
        result = result * shard_levels(own_key, extent, shards, -0.22, 0.18)
    return jnp.clip(result, -reach, reach).astype(held_as)


def setup_inputs(seed: int = 0) -> dict:
    arg_keys = jax.random.split(jax.random.key(seed), 6)
    return {
        "left_amps": normal_values(arg_keys[0], (MROWS, KW), 1.0, 6.0, ((0, 8), (1, 16))),
        "right_ints": normal_values(arg_keys[1], (KW, NCOLS), KW ** -0.5, 0.0625, ((0, 8), (1, 16))),
        "left_mask": draw_left_mask(jax.random.fold_in(arg_keys[5], 71), 0),
        "right_mask": draw_right_mask(jax.random.fold_in(arg_keys[5], 71), 0),
        "result_mask": draw_result_mask(jax.random.fold_in(arg_keys[5], 71), 0),
    }


def expand(values, mask):
    rows, cols = values.shape
    tiled = values.reshape(rows // TILE, TILE, cols // TILE, TILE)
    kept = tiled * mask.astype(values.dtype)[:, None, :, None]
    return kept.reshape(rows, cols)


def reference(left_amps, right_ints, left_mask, right_mask, result_mask):
    masked_left = expand(left_amps, left_mask)
    masked_right = expand(right_ints, right_mask)
    product = jnp.dot(masked_left, masked_right, preferred_element_type=jnp.float32)
    kept = expand(product, result_mask).astype(jnp.bfloat16)
    blocks = kept.reshape(N_ROW, ROWS_DEV, N_COL, COLS_DEV).transpose(0, 2, 1, 3)
    return blocks.reshape(N_ROW * N_COL, ROWS_DEV * COLS_DEV)
```

```python
import jax
import jax.numpy as jnp
from jax import lax
from jax.experimental import pallas as pl
from jax.experimental.pallas import tpu as pltpu
from jax.sharding import PartitionSpec as P

TILE = 128
MESH = pl.DeviceIdType.MESH
F32 = jnp.float32
BF16 = jnp.bfloat16
SIDE = 4
MIB = 1 << 20


def wrap(value, size=SIDE):
    return lax.rem(value + size, size)


def contract(
    lm_ref,
    rm_ref,
    om_ref,
    left_ref,
    right_ref,
    out_ref,
    a_buf,
    b_buf,
    a_stage,
    b_stage,
    total,
    kept,
    load_sem,
    a_send,
    a_recv,
    b_send,
    b_recv,
    x_send,
    x_recv,
    own_sem,
):
    row = lax.axis_index("row")
    col = lax.axis_index("col")
    z = row // 2
    core = lax.rem(row, 2)
    y = col // SIDE
    x = lax.rem(col, SIDE)

    load_a = pltpu.make_async_copy(left_ref, a_stage, load_sem.at[0])
    load_b = pltpu.make_async_copy(right_ref, b_stage, load_sem.at[1])
    load_a.start()
    load_b.start()

    barrier = pltpu.get_barrier_semaphore()
    me = row * 16 + col

    def greet(step, carry):
        other = lax.rem(me + step, 128)
        pl.semaphore_signal(
            barrier,
            inc=1,
            device_id=(other // 16, lax.rem(other, 16)),
            device_id_type=MESH,
        )
        return carry

    lax.fori_loop(1, 128, greet, 0)

    x_off = pl.multiple_of(x * 512, 512)
    load_a.wait()
    for j in range(4):
        for i in range(8):
            keep = lm_ref[i, j].astype(F32)
            rows = slice(i * TILE, (i + 1) * TILE)
            block = a_stage[rows, j * TILE : (j + 1) * TILE].astype(F32) * keep
            a_buf[y, rows, pl.ds(pl.multiple_of(x_off + j * TILE, TILE), TILE)] = block.astype(BF16)
    load_b.wait()
    for i in range(8):
        rows = pl.ds(pl.multiple_of(core * 1024 + i * TILE, TILE), TILE)
        for j in range(8):
            keep = rm_ref[i, j].astype(F32)
            cols = slice(j * TILE, (j + 1) * TILE)
            block = b_stage[i * TILE : (i + 1) * TILE, cols].astype(F32) * keep
            b_buf[z, rows, cols] = block.astype(BF16)

    pl.semaphore_wait(barrier, 127)

    def at(dx, dy):
        return row, wrap(y + dy) * SIDE + wrap(x + dx)

    def a_piece(half, first, second, quarter):
        dx, dy = (first, second) if half == 0 else (second, first)
        start, size = half * 512, 512
        if quarter is not None:
            start, size = start + quarter * 256, 256
        cols = pl.ds(pl.multiple_of(wrap(x + dx) * 512, 512), 512)
        return a_buf.at[wrap(y + dy), pl.ds(start, size), cols]

    def a_slot(half, first, second, side):
        f_at = {0: 0, -1: 1, 1: 2, 2: 3}
        if second == 0:
            kind = {-1: 0, 1: 1, 2: 2}[first] + (1 if first == 2 and side == 1 else 0)
        else:
            kind = 4 + 4 * f_at[first] + {-1: 0, 1: 1, 2: 2}[second]
            kind += 1 if second == 2 and side == 1 else 0
        return half * 20 + kind

    a_sent = []

    def a_go(half, first, second, axis, step, quarter):
        if axis == 0:
            there = (first - step, second)
        else:
            there = (first, second - step)
        there = tuple(2 if abs(v) == 2 else v for v in there)
        slot = a_slot(half, *there, -step)
        along_x = (axis == 0) == (half == 0)
        device = at(step, 0) if along_x else at(0, step)
        piece = a_piece(half, first, second, quarter)
        copy = pltpu.make_async_remote_copy(
            src_ref=piece,
            dst_ref=piece,
            send_sem=a_send.at[slot],
            recv_sem=a_recv.at[slot],
            device_id=device,
            device_id_type=MESH,
        )
        copy.start()
        a_sent.append(copy)

    def a_wait(half, first, second, side=0):
        quarter = None
        if first == 2 and second == 0 or second == 2:
            quarter = 0 if side == -1 else 1
        piece = a_piece(half, first, second, quarter)
        slot = a_slot(half, first, second, side)
        pltpu.make_async_copy(piece, piece, a_recv.at[slot]).wait()

    def b_piece(dz, side, half):
        start = pl.multiple_of(side * 1024 + (0 if half is None else half * 512), 512)
        return b_buf.at[wrap(z + dz), pl.ds(start, 1024 if half is None else 512), :]

    b_sent = []

    def b_go(dz, half, step, slot):
        piece = b_piece(dz, core, half)
        device = (wrap(z + step) * 2 + core, col) if step else (z * 2 + 1 - core, col)
        copy = pltpu.make_async_remote_copy(
            src_ref=piece,
            dst_ref=piece,
            send_sem=b_send.at[slot],
            recv_sem=b_recv.at[slot],
            device_id=device,
            device_id_type=MESH,
        )
        copy.start()
        b_sent.append(copy)

    def b_wait(dz, half, slot, other=False):
        piece = b_piece(dz, 1 - core if other else core, half)
        pltpu.make_async_copy(piece, piece, b_recv.at[slot]).wait()

    halves = (0, 1)
    steps = (1, -1)
    for step in steps:
        for half in halves:
            a_go(half, 0, 0, 0, step, None)
    b_go(0, 0, 1, 0)
    b_go(0, 1, -1, 1)
    b_go(0, 1, 1, 2)
    b_go(0, 0, -1, 3)
    for step in steps:
        for half in halves:
            a_go(half, 0, 0, 1, step, None)
    b_go(0, None, 0, 6)

    for half in halves:
        a_wait(half, -1, 0)
        a_go(half, -1, 0, 0, 1, 0)
        a_wait(half, 1, 0)
        a_go(half, 1, 0, 0, -1, 1)
    for first in (-1, 1):
        for half in halves:
            for step in steps:
                a_go(half, first, 0, 1, step, None)

    def relay(first):
        for half in halves:
            a_wait(half, first, -1)
            a_go(half, first, -1, 1, 1, 0)
            a_wait(half, first, 1)
            a_go(half, first, 1, 1, -1, 1)

    relay(0)
    b_wait(-1, 0, 0)
    b_go(-1, 0, 1, 4)
    b_wait(1, 1, 1)
    b_go(1, 1, -1, 5)
    b_go(-1, 0, 0, 7)
    b_go(1, 1, 0, 8)
    for half in halves:
        a_wait(half, 2, 0, -1)
        a_wait(half, 2, 0, 1)
        for step in steps:
            a_go(half, 2, 0, 1, step, None)
    relay(-1)
    b_wait(-1, 1, 2)
    b_go(-1, 1, 0, 9)
    b_wait(1, 0, 3)
    b_go(1, 0, 0, 10)
    relay(1)
    relay(2)
    b_wait(2, 0, 4)
    b_go(2, 0, 0, 11)
    b_wait(2, 1, 5)
    b_go(2, 1, 0, 12)

    b_wait(0, None, 6, True)
    b_wait(-1, 0, 7, True)
    b_wait(1, 1, 8, True)
    b_wait(-1, 1, 9, True)
    b_wait(1, 0, 10, True)
    b_wait(2, 0, 11, True)
    b_wait(2, 1, 12, True)

    def a_end(half, first):
        a_wait(half, first, 2, -1)
        a_wait(half, first, 2, 1)

    def add(half, dy, fresh):
        group = wrap(y + dy)
        rows = pl.ds(half * 512, 512)

        def one(n, carry):
            cols = pl.ds(pl.multiple_of(n * 256, 256), 256)
            part = jnp.dot(a_buf[group, rows, :], b_buf[group, :, cols], preferred_element_type=F32)
            if fresh:
                total[rows, cols] = part
            else:
                total[rows, cols] += part
            return carry

        lax.fori_loop(0, 4, one, 0)

    add(0, 0, True)
    add(0, -1, False)
    add(0, 1, False)
    a_end(1, 0)
    add(1, 0, True)
    a_end(1, -1)
    add(1, -1, False)
    a_end(1, 1)
    add(1, 1, False)
    a_end(1, 2)
    for first in (0, -1, 1, 2):
        a_end(0, first)

    last = wrap(y + 2)
    order = (2, 1, 3, 0)

    def finish(dz):
        quarter = wrap(z + dz)
        rows = pl.ds(pl.multiple_of(quarter * 256, 256), 256)

        def one(n, carry):
            cols = pl.ds(pl.multiple_of(n * 256, 256), 256)
            part = total[rows, cols] + jnp.dot(
                a_buf[last, rows, :], b_buf[last, :, cols], preferred_element_type=F32
            )
            for i in range(2):
                for j in range(2):
                    keep = om_ref[quarter * 2 + i, n * 2 + j].astype(F32)
                    block = part[i * TILE : (i + 1) * TILE, j * TILE : (j + 1) * TILE] * keep
                    kept[
                        pl.ds(quarter * 32 + i * 16, 16),
                        :,
                        pl.ds(pl.multiple_of(n * 256 + j * TILE, TILE), TILE),
                    ] = block.reshape(16, 8, TILE).astype(BF16)
            return carry

        lax.fori_loop(0, 4, one, 0)

    def hand_out(dz):
        quarter = wrap(z + dz)

        def one(t, carry):
            to_core = lax.rem(core + t // 16, 2)
            to_y = wrap(y + lax.rem(t // 4, 4))
            to_x = wrap(x + lax.rem(t, 4))
            to_row = quarter * 2 + to_core
            to_col = to_y * 4 + to_x
            pltpu.make_async_remote_copy(
                src_ref=kept.at[to_row * 16 + to_col],
                dst_ref=out_ref.at[me],
                send_sem=x_send,
                recv_sem=x_recv,
                device_id=(to_row, to_col),
                device_id_type=MESH,
            ).start()
            return carry

        lax.fori_loop(1 if dz == 0 else 0, 32, one, 0)

    finish(order[0])
    for now, later in zip(order, order[1:]):
        finish(later)
        hand_out(now)
    hand_out(order[-1])
    own = pltpu.make_async_copy(kept.at[me], out_ref.at[me], own_sem)
    own.start()

    for copy in a_sent + b_sent:
        copy.wait_send()
    own.wait()
    pltpu.make_async_copy(kept.at[pl.ds(0, 127)], kept.at[pl.ds(0, 127)], x_send).wait()
    pltpu.make_async_copy(out_ref.at[pl.ds(0, 127)], out_ref.at[pl.ds(0, 127)], x_recv).wait()


def flatten_kernel(in_ref, out_ref):
    block = in_ref[...].astype(F32)
    turned = jnp.swapaxes(block, 0, 1)
    for a in range(8):
        out_ref[:, a * 1024 : (a + 1) * 1024] = turned[a].astype(BF16)


def local(left_amps, right_ints, left_mask, right_mask, result_mask):
    smem = pl.BlockSpec(memory_space=pltpu.SMEM)
    hbm = pl.BlockSpec(memory_space=pl.ANY)
    strips = pl.pallas_call(
        contract,
        out_shape=jax.ShapeDtypeStruct((128, 8, 1024), BF16),
        in_specs=[smem, smem, smem, hbm, hbm],
        out_specs=hbm,
        scratch_shapes=[
            pltpu.VMEM((4, 1024, 2048), BF16),
            pltpu.VMEM((4, 2048, 1024), BF16),
            pltpu.VMEM((1024, 512), BF16),
            pltpu.VMEM((1024, 1024), BF16),
            pltpu.VMEM((1024, 1024), F32),
            pltpu.VMEM((128, 8, 1024), BF16),
            pltpu.SemaphoreType.DMA((2,)),
            pltpu.SemaphoreType.DMA((40,)),
            pltpu.SemaphoreType.DMA((40,)),
            pltpu.SemaphoreType.DMA((13,)),
            pltpu.SemaphoreType.DMA((13,)),
            pltpu.SemaphoreType.DMA(()),
            pltpu.SemaphoreType.DMA(()),
            pltpu.SemaphoreType.DMA(()),
        ],
        compiler_params=pltpu.CompilerParams(
            collective_id=0, has_side_effects=True, vmem_limit_bytes=60 * MIB
        ),
        name="contract",
    )(left_mask, right_mask, result_mask, left_amps, right_ints)
    return pl.pallas_call(
        flatten_kernel,
        grid=(8,),
        in_specs=[pl.BlockSpec((16, 8, 1024), lambda p: (p, 0, 0))],
        out_specs=pl.BlockSpec((16, 8192), lambda p: (p, 0)),
        out_shape=jax.ShapeDtypeStruct((128, 8192), BF16),
        name="flatten",
    )(strips)


def solution(mesh):
    in_specs = (P("row", "col"), P("row", "col"), P("row", "col"), P("row", "col"), P("row", "col"))
    out_specs = P(None, ("row", "col"))
    return jax.shard_map(local, mesh=mesh, in_specs=in_specs, out_specs=out_specs, check_vma=False)
```

```python
import jax
import jax.numpy as jnp
from jax import lax
from jax.experimental import pallas as pl
from jax.experimental.pallas import tpu as pltpu
from jax.sharding import PartitionSpec as P

TILE = 128
MESH = pl.DeviceIdType.MESH
F32 = jnp.float32
BF16 = jnp.bfloat16
SIDE = 4
MIB = 1 << 20


def wrap(value, size=SIDE):
    return lax.rem(value + size, size)


def contract(
    lm_ref,
    rm_ref,
    om_ref,
    left_ref,
    right_ref,
    out_ref,
    a_buf,
    b_buf,
    a_stage,
    b_stage,
    total,
    kept,
    load_sem,
    a_send,
    a_recv,
    b_send,
    b_recv,
    x_send,
    x_recv,
    own_sem,
    round_sem,
):
    row = lax.axis_index("row")
    col = lax.axis_index("col")
    z = row // 2
    core = lax.rem(row, 2)
    y = col // SIDE
    x = lax.rem(col, SIDE)

    load_a = pltpu.make_async_copy(left_ref, a_stage, load_sem.at[0])
    load_b = pltpu.make_async_copy(right_ref, b_stage, load_sem.at[1])
    load_a.start()
    load_b.start()

    barrier = pltpu.get_barrier_semaphore()
    me = row * 16 + col

    def at(dx, dy):
        return row, wrap(y + dy) * SIDE + wrap(x + dx)

    def along_z(step):
        return wrap(z + step) * 2 + core, col

    x_side = (at(1, 0), at(-1, 0))
    y_side = (at(0, 1), at(0, -1))
    z_side = (along_z(1), along_z(-1))
    mate = (z * 2 + 1 - core, col)

    def greet(sem, devices):
        for device in devices:
            pl.semaphore_signal(sem, inc=1, device_id=device, device_id_type=MESH)

    greet(barrier, (*x_side, *y_side, *z_side, mate))

    x_off = pl.multiple_of(x * 512, 512)
    load_a.wait()
    for j in range(4):
        for i in range(8):
            keep = lm_ref[j, i].astype(F32)
            rows = slice(i * TILE, (i + 1) * TILE)
            block = a_stage[rows, j * TILE : (j + 1) * TILE].astype(F32) * keep
            a_buf[y, rows, pl.ds(pl.multiple_of(x_off + j * TILE, TILE), TILE)] = block.astype(BF16)
    load_b.wait()
    for i in range(8):
        rows = pl.ds(pl.multiple_of(core * 1024 + i * TILE, TILE), TILE)
        for j in range(8):
            keep = rm_ref[i, j].astype(F32)
            cols = slice(j * TILE, (j + 1) * TILE)
            block = b_stage[i * TILE : (i + 1) * TILE, cols].astype(F32) * keep
            b_buf[z, rows, cols] = block.astype(BF16)

    pl.semaphore_wait(barrier, 7)

    rounds = (x_side, y_side, y_side, z_side, z_side, (mate,))

    def pass_on(step):
        if step > 0:
            pl.semaphore_wait(round_sem.at[step - 1], len(rounds[step - 1]))
        if step < len(rounds):
            greet(round_sem.at[step], rounds[step])


    def a_piece(half, first, second, quarter):
        dx, dy = (first, second) if half == 0 else (second, first)
        start, size = half * 512, 512
        if quarter is not None:
            start, size = start + quarter * 256, 256
        cols = pl.ds(pl.multiple_of(wrap(x + dx) * 512, 512), 512)
        return a_buf.at[wrap(y + dy), pl.ds(start, size), cols]

    def a_slot(half, first, second, side):
        f_at = {0: 0, -1: 1, 1: 2, 2: 3}
        if second == 0:
            kind = {-1: 0, 1: 1, 2: 2}[first] + (1 if first == 2 and side == 1 else 0)
        else:
            kind = 4 + 4 * f_at[first] + {-1: 0, 1: 1, 2: 2}[second]
            kind += 1 if second == 2 and side == 1 else 0
        return half * 20 + kind

    a_sent = []

    def a_go(half, first, second, axis, step, quarter):
        if axis == 0:
            there = (first - step, second)
        else:
            there = (first, second - step)
        there = tuple(2 if abs(v) == 2 else v for v in there)
        slot = a_slot(half, *there, -step)
        along_x = (axis == 0) == (half == 0)
        device = at(step, 0) if along_x else at(0, step)
        piece = a_piece(half, first, second, quarter)
        copy = pltpu.make_async_remote_copy(
            src_ref=piece,
            dst_ref=piece,
            send_sem=a_send.at[slot],
            recv_sem=a_recv.at[slot],
            device_id=device,
            device_id_type=MESH,
        )
        copy.start()
        a_sent.append(copy)

    def a_wait(half, first, second, side=0):
        quarter = None
        if first == 2 and second == 0 or second == 2:
            quarter = 0 if side == -1 else 1
        piece = a_piece(half, first, second, quarter)
        slot = a_slot(half, first, second, side)
        pltpu.make_async_copy(piece, piece, a_recv.at[slot]).wait()

    def a_end(half, first):
        a_wait(half, first, 2, -1)
        a_wait(half, first, 2, 1)

    near = wrap(y - z)

    def b_piece(dz, side, piece, count=1):
        start = pl.multiple_of(side * 1024 + piece * 256, 256)
        return b_buf.at[wrap(z + dz), pl.ds(start, 256 * count), :]

    def b_go(dz, piece, step, count=1):
        if step and dz == 0:
            slot = piece + (0 if step == 1 else 4)
        elif step:
            slot = 8 + piece
        else:
            slot = {0: 12, -1: 13, 1: 17, 2: 21}[dz] + piece
        part = b_piece(dz, core, piece, count)
        device = (wrap(z + step) * 2 + core, col) if step else (z * 2 + 1 - core, col)
        pltpu.make_async_remote_copy(
            src_ref=part,
            dst_ref=part,
            send_sem=b_send.at[slot],
            recv_sem=b_recv.at[slot],
            device_id=device,
            device_id_type=MESH,
        ).start()

    def b_wait(dz, piece, other=False, count=1):
        if other:
            slot = {0: 12, -1: 13, 1: 17, 2: 21}[dz] + piece
        else:
            slot = {-1: 0, 1: 4, 2: 8}[dz] + piece
        part = b_piece(dz, 1 - core if other else core, piece, count)
        pltpu.make_async_copy(part, part, b_recv.at[slot]).wait()

    def b_relay(dz, piece):
        b_wait(dz, piece)
        b_go(dz, piece, -dz)
        b_go(dz, piece, 0)

    def b_rest(dz):
        for piece in {0: (), -1: (2, 3), 1: (1, 0), 2: (0, 3, 1, 2)}[dz]:
            b_wait(dz, piece)
            b_go(dz, piece, 0)
        if dz == 0:
            b_wait(0, 0, True, 4)
        else:
            for piece in range(4):
                b_wait(dz, piece, True)

    up, down = (0, 1, 2, 3), (3, 2, 1, 0)

    def own_up():
        for piece in up[1:]:
            b_go(0, piece, 1)

    def own_down():
        for piece in down[1:]:
            b_go(0, piece, -1)

    halves = (0, 1)
    steps = (1, -1)
    for step in steps:
        for half in halves:
            a_go(half, 0, 0, 0, step, None)
    b_go(0, up[0], 1)
    b_go(0, down[0], -1)
    pl.when(near != 3)(own_up)
    pl.when(near != 1)(own_down)
    for step in steps:
        for half in halves:
            a_go(half, 0, 0, 1, step, None)
    b_go(0, 0, 0, 4)
    pass_on(0)

    for half in halves:
        a_wait(half, -1, 0)
        a_go(half, -1, 0, 0, 1, 0)
        a_wait(half, 1, 0)
        a_go(half, 1, 0, 0, -1, 1)
    for first in (-1, 1):
        for half in halves:
            for step in steps:
                a_go(half, first, 0, 1, step, None)
    pass_on(1)
    b_relay(-1, 0)
    b_relay(1, 3)
    pass_on(2)

    def relay(first):
        for half in halves:
            a_wait(half, first, -1)
            a_go(half, first, -1, 1, 1, 0)
            a_wait(half, first, 1)
            a_go(half, first, 1, 1, -1, 1)

    relay(0)

    def second_relays():
        b_relay(-1, 1)
        b_relay(1, 2)

    pl.when(near != 2)(second_relays)
    pl.when(near == 3)(own_up)
    pl.when(near == 1)(own_down)
    pass_on(3)
    for half in halves:
        a_wait(half, 2, 0, -1)
        a_wait(half, 2, 0, 1)
        for step in steps:
            a_go(half, 2, 0, 1, step, None)
    pass_on(4)
    relay(-1)
    pass_on(5)
    pl.when(near == 2)(second_relays)
    for dz in (0, 1, 2, -1):
        pl.when(near == dz % SIDE)(lambda dz=dz: b_rest(dz))

    def add(half, dy, fresh):
        group = wrap(y + dy)
        rows = pl.ds(half * 512, 512)

        def one(n, carry):
            cols = pl.ds(pl.multiple_of(n * 256, 256), 256)
            part = jnp.dot(a_buf[group, rows, :], b_buf[group, :, cols], preferred_element_type=F32)
            if fresh:
                total[rows, cols] = part
            else:
                total[rows, cols] += part
            return carry

        lax.fori_loop(0, 4, one, 0)

    add(0, 0, True)
    relay(1)
    pass_on(6)
    a_end(1, 0)
    add(1, 0, True)
    relay(2)
    for dz in (0, 1, -1, 2):
        pl.when(near != dz % SIDE)(lambda dz=dz: b_rest(dz))

    add(0, -1, False)
    a_end(1, -1)
    add(1, -1, False)
    a_end(1, 1)
    a_end(1, 2)
    for first in (0, -1, 1, 2):
        a_end(0, first)

    order = (0, 1, 3, 2)

    def strips_of(part):
        found = []
        for dz in range(SIDE):
            there_y = wrap(y + (part - dz) % SIDE)
            for there_core in range(2):
                found.append((wrap(z + dz) * 2 + there_core, there_y))
        return found

    def finish(part):
        strips = strips_of(part)
        rows = [pl.ds(pl.multiple_of(g * TILE + v * 32, 32), 32) for g, v in strips]

        def one(n, carry):
            cols = pl.ds(pl.multiple_of(n * 256, 256), 256)
            value = jnp.concatenate([total[r, cols] for r in rows], axis=0)
            for dy in (1, 2):
                group = wrap(y + dy)
                lhs = jnp.concatenate([a_buf[group, r, :] for r in rows], axis=0)
                value += jnp.dot(lhs, b_buf[group, :, cols], preferred_element_type=F32)
            for i, (g, v) in enumerate(strips):
                for j in range(2):
                    keep = om_ref[g, n * 2 + j].astype(F32)
                    block = value[i * 32 : (i + 1) * 32, j * TILE : (j + 1) * TILE] * keep
                    kept[
                        pl.ds(g * 16 + v * 4, 4),
                        :,
                        pl.ds(pl.multiple_of(n * 256 + j * TILE, TILE), TILE),
                    ] = block.reshape(4, 8, TILE).astype(BF16)
            return carry

        lax.fori_loop(0, 4, one, 0)

    def hand_out(part):
        def one(t, carry):
            dz = lax.rem(t, 4)
            to_row = wrap(z + dz) * 2 + lax.rem(core + t // 16, 2)
            to_y = lax.rem(y + part + 4 - dz, 4)
            to_col = to_y * 4 + lax.rem(x + t + t // 4, 4)
            pltpu.make_async_remote_copy(
                src_ref=kept.at[to_row * 16 + to_col],
                dst_ref=out_ref.at[me],
                send_sem=x_send,
                recv_sem=x_recv,
                device_id=(to_row, to_col),
                device_id_type=MESH,
            ).start()
            return carry

        lax.fori_loop(1 if part == 0 else 0, 32, one, 0)

    finish(order[0])
    for now, later in zip(order, order[1:]):
        finish(later)
        hand_out(now)
    hand_out(order[-1])
    own = pltpu.make_async_copy(kept.at[me], out_ref.at[me], own_sem)
    own.start()

    for copy in a_sent:
        copy.wait_send()
    for slot in range(25):
        part = b_piece(0, core, 0, 4 if slot == 12 else 1)
        pltpu.make_async_copy(part, part, b_send.at[slot]).wait()
    own.wait()
    pltpu.make_async_copy(kept.at[pl.ds(0, 127)], kept.at[pl.ds(0, 127)], x_send).wait()
    pltpu.make_async_copy(out_ref.at[pl.ds(0, 127)], out_ref.at[pl.ds(0, 127)], x_recv).wait()


def flatten_kernel(in_ref, out_ref):
    out_ref[...] = in_ref[...].reshape(out_ref.shape)


def local(left_amps, right_ints, left_mask, right_mask, result_mask):
    smem = pl.BlockSpec(memory_space=pltpu.SMEM)
    hbm = pl.BlockSpec(memory_space=pl.ANY)
    strips = pl.pallas_call(
        contract,
        out_shape=jax.ShapeDtypeStruct((128, 8, 1024), BF16),
        in_specs=[smem, smem, smem, hbm, hbm],
        out_specs=hbm,
        scratch_shapes=[
            pltpu.VMEM((4, 1024, 2048), BF16),
            pltpu.VMEM((4, 2048, 1024), BF16),
            pltpu.VMEM((1024, 512), BF16),
            pltpu.VMEM((1024, 1024), BF16),
            pltpu.VMEM((1024, 1024), F32),
            pltpu.VMEM((128, 8, 1024), BF16),
            pltpu.SemaphoreType.DMA((2,)),
            pltpu.SemaphoreType.DMA((40,)),
            pltpu.SemaphoreType.DMA((40,)),
            pltpu.SemaphoreType.DMA((25,)),
            pltpu.SemaphoreType.DMA((25,)),
            pltpu.SemaphoreType.DMA(()),
            pltpu.SemaphoreType.DMA(()),
            pltpu.SemaphoreType.DMA(()),
            pltpu.SemaphoreType.REGULAR((6,)),
        ],
        compiler_params=pltpu.CompilerParams(
            collective_id=0, has_side_effects=True, vmem_limit_bytes=60 * MIB
        ),
        name="contract",
    )(left_mask.T, right_mask, result_mask, left_amps, right_ints)
    return pl.pallas_call(
        flatten_kernel,
        grid=(2,),
        in_specs=[pl.BlockSpec((64, 8, 1024), lambda p: (p, 0, 0))],
        out_specs=pl.BlockSpec((64, 8192), lambda p: (p, 0)),
        out_shape=jax.ShapeDtypeStruct((128, 8192), BF16),
        name="flatten",
    )(strips)


def solution(mesh):
    in_specs = (P("row", "col"), P("row", "col"), P("row", "col"), P("row", "col"), P("row", "col"))
    out_specs = P(None, ("row", "col"))
    return jax.shard_map(local, mesh=mesh, in_specs=in_specs, out_specs=out_specs, check_vma=False)
```

```python
import jax
import jax.numpy as jnp
from jax import lax
from jax.experimental import pallas as pl
from jax.experimental.pallas import tpu as pltpu
from jax.sharding import PartitionSpec as P

TILE = 128
MESH = pl.DeviceIdType.MESH
F32 = jnp.float32
BF16 = jnp.bfloat16
SIDE = 4
MIB = 1 << 20


def wrap(value, size=SIDE):
    return lax.rem(value + size, size)


def contract(
    lm_ref,
    rm_ref,
    om_ref,
    left_ref,
    right_ref,
    out_ref,
    a_buf,
    b_buf,
    a_stage,
    b_stage,
    total,
    kept,
    load_sem,
    a_send,
    a_recv,
    b_send,
    b_recv,
    x_send,
    x_recv,
    own_sem,
    round_sem,
):
    row = lax.axis_index("row")
    col = lax.axis_index("col")
    z = row // 2
    core = lax.rem(row, 2)
    y = col // SIDE
    x = lax.rem(col, SIDE)

    load_a = pltpu.make_async_copy(left_ref, a_stage, load_sem.at[0])
    load_b = pltpu.make_async_copy(right_ref, b_stage, load_sem.at[1])
    load_a.start()
    load_b.start()

    barrier = pltpu.get_barrier_semaphore()
    me = row * 16 + col

    def at(dx, dy):
        return row, wrap(y + dy) * SIDE + wrap(x + dx)

    def along_z(step):
        return wrap(z + step) * 2 + core, col

    x_side = (at(1, 0), at(-1, 0))
    y_side = (at(0, 1), at(0, -1))
    z_side = (along_z(1), along_z(-1))
    mate = (z * 2 + 1 - core, col)

    def greet(sem, devices):
        for device in devices:
            pl.semaphore_signal(sem, inc=1, device_id=device, device_id_type=MESH)

    greet(barrier, (*x_side, *y_side, *z_side, mate))

    x_off = pl.multiple_of(x * 512, 512)
    load_a.wait()
    for j in range(4):
        for i in range(8):
            keep = lm_ref[j, i].astype(F32)
            rows = slice(i * TILE, (i + 1) * TILE)
            block = a_stage[rows, j * TILE : (j + 1) * TILE].astype(F32) * keep
            a_buf[y, rows, pl.ds(pl.multiple_of(x_off + j * TILE, TILE), TILE)] = block.astype(BF16)
    load_b.wait()
    for i in range(8):
        rows = pl.ds(pl.multiple_of(core * 1024 + i * TILE, TILE), TILE)
        for j in range(8):
            keep = rm_ref[i, j].astype(F32)
            cols = slice(j * TILE, (j + 1) * TILE)
            block = b_stage[i * TILE : (i + 1) * TILE, cols].astype(F32) * keep
            b_buf[z, rows, cols] = block.astype(BF16)

    pl.semaphore_wait(barrier, 7)

    rounds = (x_side, y_side, y_side, z_side, z_side, (mate,))

    def pass_on(step):
        if step > 0:
            pl.semaphore_wait(round_sem.at[step - 1], len(rounds[step - 1]))
        if step < len(rounds):
            greet(round_sem.at[step], rounds[step])


    def a_piece(half, first, second, quarter):
        dx, dy = (first, second) if half == 0 else (second, first)
        start, size = half * 512, 512
        if quarter is not None:
            start, size = start + quarter * 256, 256
        cols = pl.ds(pl.multiple_of(wrap(x + dx) * 512, 512), 512)
        return a_buf.at[wrap(y + dy), pl.ds(start, size), cols]

    def a_slot(half, first, second, side):
        f_at = {0: 0, -1: 1, 1: 2, 2: 3}
        if second == 0:
            kind = {-1: 0, 1: 1, 2: 2}[first] + (1 if first == 2 and side == 1 else 0)
        else:
            kind = 4 + 4 * f_at[first] + {-1: 0, 1: 1, 2: 2}[second]
            kind += 1 if second == 2 and side == 1 else 0
        return half * 20 + kind

    a_sent = []

    def a_go(half, first, second, axis, step, quarter):
        if axis == 0:
            there = (first - step, second)
        else:
            there = (first, second - step)
        there = tuple(2 if abs(v) == 2 else v for v in there)
        slot = a_slot(half, *there, -step)
        along_x = (axis == 0) == (half == 0)
        device = at(step, 0) if along_x else at(0, step)
        piece = a_piece(half, first, second, quarter)
        copy = pltpu.make_async_remote_copy(
            src_ref=piece,
            dst_ref=piece,
            send_sem=a_send.at[slot],
            recv_sem=a_recv.at[slot],
            device_id=device,
            device_id_type=MESH,
        )
        copy.start()
        a_sent.append(copy)

    def a_wait(half, first, second, side=0):
        quarter = None
        if first == 2 and second == 0 or second == 2:
            quarter = 0 if side == -1 else 1
        piece = a_piece(half, first, second, quarter)
        slot = a_slot(half, first, second, side)
        pltpu.make_async_copy(piece, piece, a_recv.at[slot]).wait()

    def a_end(half, first):
        a_wait(half, first, 2, -1)
        a_wait(half, first, 2, 1)

    near = wrap(y - z)

    def b_piece(dz, side, piece, count=1):
        start = pl.multiple_of(side * 1024 + piece * 256, 256)
        return b_buf.at[wrap(z + dz), pl.ds(start, 256 * count), :]

    def b_go(dz, piece, step, count=1):
        if step and dz == 0:
            slot = piece + (0 if step == 1 else 4)
        elif step:
            slot = 8 + piece
        else:
            slot = {0: 12, -1: 13, 1: 17, 2: 21}[dz] + piece
        part = b_piece(dz, core, piece, count)
        device = (wrap(z + step) * 2 + core, col) if step else (z * 2 + 1 - core, col)
        pltpu.make_async_remote_copy(
            src_ref=part,
            dst_ref=part,
            send_sem=b_send.at[slot],
            recv_sem=b_recv.at[slot],
            device_id=device,
            device_id_type=MESH,
        ).start()

    def b_wait(dz, piece, other=False, count=1):
        if other:
            slot = {0: 12, -1: 13, 1: 17, 2: 21}[dz] + piece
        else:
            slot = {-1: 0, 1: 4, 2: 8}[dz] + piece
        part = b_piece(dz, 1 - core if other else core, piece, count)
        pltpu.make_async_copy(part, part, b_recv.at[slot]).wait()

    def b_relay(dz, piece):
        b_wait(dz, piece)
        b_go(dz, piece, -dz)
        b_go(dz, piece, 0)

    def b_rest(dz):
        for piece in {0: (), -1: (2, 3), 1: (1, 0), 2: (0, 3, 1, 2)}[dz]:
            b_wait(dz, piece)
            b_go(dz, piece, 0)
        if dz == 0:
            b_wait(0, 0, True, 4)
        else:
            for piece in range(4):
                b_wait(dz, piece, True)

    up, down = (0, 1, 2, 3), (3, 2, 1, 0)

    def own_up():
        for piece in up[1:]:
            b_go(0, piece, 1)

    def own_down():
        for piece in down[1:]:
            b_go(0, piece, -1)

    halves = (0, 1)
    steps = (1, -1)
    for step in steps:
        for half in halves:
            a_go(half, 0, 0, 0, step, None)
    b_go(0, up[0], 1)
    b_go(0, down[0], -1)
    pl.when(near != 3)(own_up)
    pl.when(near != 1)(own_down)
    for step in steps:
        for half in halves:
            a_go(half, 0, 0, 1, step, None)
    b_go(0, 0, 0, 4)
    pass_on(0)

    for half in halves:
        a_wait(half, -1, 0)
        a_go(half, -1, 0, 0, 1, 0)
        a_wait(half, 1, 0)
        a_go(half, 1, 0, 0, -1, 1)
    for first in (-1, 1):
        for half in halves:
            for step in steps:
                a_go(half, first, 0, 1, step, None)
    pass_on(1)
    b_relay(-1, 0)
    b_relay(1, 3)
    pass_on(2)

    def relay(first):
        for half in halves:
            a_wait(half, first, -1)
            a_go(half, first, -1, 1, 1, 0)
            a_wait(half, first, 1)
            a_go(half, first, 1, 1, -1, 1)

    relay(0)

    def second_relays():
        b_relay(-1, 1)
        b_relay(1, 2)

    pl.when(near != 2)(second_relays)
    pl.when(near == 3)(own_up)
    pl.when(near == 1)(own_down)
    pass_on(3)
    for half in halves:
        a_wait(half, 2, 0, -1)
        a_wait(half, 2, 0, 1)
        for step in steps:
            a_go(half, 2, 0, 1, step, None)
    pass_on(4)
    relay(-1)
    pass_on(5)
    pl.when(near == 2)(second_relays)
    for dz in (0, 1, 2, -1):
        pl.when(near == dz % SIDE)(lambda dz=dz: b_rest(dz))

    def depth(dx):
        return pl.ds(pl.multiple_of(wrap(x + dx) * 512, 512), 512)

    def add(half, blocks, fresh=False):
        rows = pl.ds(half * 512, 512)
        width = 512 if blocks[0][1] is None else 1024

        def one(n, carry):
            cols = pl.ds(pl.multiple_of(n * width, width), width)
            part = None
            for dy, dx in blocks:
                group, k = wrap(y + dy), slice(None) if dx is None else depth(dx)
                term = jnp.dot(a_buf[group, rows, k], b_buf[group, k, cols], preferred_element_type=F32)
                part = term if part is None else part + term
            if fresh:
                total[rows, cols] = part
            else:
                total[rows, cols] += part
            return carry

        lax.fori_loop(0, 1024 // width, one, 0)

    close = (0, -1, 1)
    add(0, [(0, None)], True)
    relay(1)
    pass_on(6)
    a_end(1, 0)
    add(1, [(0, None)], True)
    for dz in (0, 1, -1, 2):
        pl.when(near != dz % SIDE)(lambda dz=dz: b_rest(dz))
    for dy in (-1, 1):
        for half in halves:
            add(half, [(dy, dx) for dx in close])
    relay(2)
    add(1, [(2, dx) for dx in close])
    for first in close:
        a_end(0, first)
    add(0, [(2, dx) for dx in close] + [(-1, 2), (1, 2)])
    a_end(1, -1)
    a_end(1, 1)
    add(1, [(-1, 2), (1, 2)])
    a_end(1, 2)
    a_end(0, 2)

    order = (0, 1, 3, 2)

    def strips_of(part):
        found = []
        for dz in range(SIDE):
            there_y = wrap(y + (part - dz) % SIDE)
            for there_core in range(2):
                found.append((wrap(z + dz) * 2 + there_core, there_y))
        return found

    def finish(part):
        strips = strips_of(part)
        rows = [pl.ds(pl.multiple_of(g * TILE + v * 32, 32), 32) for g, v in strips]
        group, k = wrap(y + 2), depth(2)

        value = jnp.concatenate([total[r, :] for r in rows], axis=0)
        lhs = jnp.concatenate([a_buf[group, r, k] for r in rows], axis=0)
        value += jnp.dot(lhs, b_buf[group, k, :], preferred_element_type=F32)
        for i, (g, v) in enumerate(strips):
            for j in range(8):
                keep = om_ref[g, j].astype(F32)
                block = value[i * 32 : (i + 1) * 32, j * TILE : (j + 1) * TILE] * keep
                kept[pl.ds(g * 16 + v * 4, 4), :, j * TILE : (j + 1) * TILE] = block.reshape(
                    4, 8, TILE
                ).astype(BF16)

    def hand_out(part):
        def one(t, carry):
            dz = lax.rem(t, 4)
            to_row = wrap(z + dz) * 2 + lax.rem(core + t // 16, 2)
            to_y = lax.rem(y + part + 4 - dz, 4)
            to_col = to_y * 4 + lax.rem(x + t + t // 4, 4)
            pltpu.make_async_remote_copy(
                src_ref=kept.at[to_row * 16 + to_col],
                dst_ref=out_ref.at[me],
                send_sem=x_send,
                recv_sem=x_recv,
                device_id=(to_row, to_col),
                device_id_type=MESH,
            ).start()
            return carry

        lax.fori_loop(1 if part == 0 else 0, 32, one, 0)

    finish(order[0])
    for now, later in zip(order, order[1:]):
        finish(later)
        hand_out(now)
    hand_out(order[-1])
    own = pltpu.make_async_copy(kept.at[me], out_ref.at[me], own_sem)
    own.start()

    for copy in a_sent:
        copy.wait_send()
    for slot in range(25):
        part = b_piece(0, core, 0, 4 if slot == 12 else 1)
        pltpu.make_async_copy(part, part, b_send.at[slot]).wait()
    own.wait()
    pltpu.make_async_copy(kept.at[pl.ds(0, 127)], kept.at[pl.ds(0, 127)], x_send).wait()
    pltpu.make_async_copy(out_ref.at[pl.ds(0, 127)], out_ref.at[pl.ds(0, 127)], x_recv).wait()


def flatten_kernel(in_ref, out_ref):
    out_ref[...] = in_ref[...].reshape(out_ref.shape)


def local(left_amps, right_ints, left_mask, right_mask, result_mask):
    smem = pl.BlockSpec(memory_space=pltpu.SMEM)
    hbm = pl.BlockSpec(memory_space=pl.ANY)
    strips = pl.pallas_call(
        contract,
        out_shape=jax.ShapeDtypeStruct((128, 8, 1024), BF16),
        in_specs=[smem, smem, smem, hbm, hbm],
        out_specs=hbm,
        scratch_shapes=[
            pltpu.VMEM((4, 1024, 2048), BF16),
            pltpu.VMEM((4, 2048, 1024), BF16),
            pltpu.VMEM((1024, 512), BF16),
            pltpu.VMEM((1024, 1024), BF16),
            pltpu.VMEM((1024, 1024), F32),
            pltpu.VMEM((128, 8, 1024), BF16),
            pltpu.SemaphoreType.DMA((2,)),
            pltpu.SemaphoreType.DMA((40,)),
            pltpu.SemaphoreType.DMA((40,)),
            pltpu.SemaphoreType.DMA((25,)),
            pltpu.SemaphoreType.DMA((25,)),
            pltpu.SemaphoreType.DMA(()),
            pltpu.SemaphoreType.DMA(()),
            pltpu.SemaphoreType.DMA(()),
            pltpu.SemaphoreType.REGULAR((6,)),
        ],
        compiler_params=pltpu.CompilerParams(
            collective_id=0, has_side_effects=True, vmem_limit_bytes=60 * MIB
        ),
        name="contract",
    )(left_mask.T, right_mask, result_mask, left_amps, right_ints)
    return pl.pallas_call(
        flatten_kernel,
        grid=(2,),
        in_specs=[pl.BlockSpec((64, 8, 1024), lambda p: (p, 0, 0))],
        out_specs=pl.BlockSpec((64, 8192), lambda p: (p, 0)),
        out_shape=jax.ShapeDtypeStruct((128, 8192), BF16),
        name="flatten",
    )(strips)


def solution(mesh):
    in_specs = (P("row", "col"), P("row", "col"), P("row", "col"), P("row", "col"), P("row", "col"))
    out_specs = P(None, ("row", "col"))
    return jax.shard_map(local, mesh=mesh, in_specs=in_specs, out_specs=out_specs, check_vma=False)
```

```python
import jax
import jax.numpy as jnp
from jax import lax
from jax.experimental import pallas as pl
from jax.experimental.pallas import tpu as pltpu
from jax.sharding import PartitionSpec as P

TILE = 128
MESH = pl.DeviceIdType.MESH
F32 = jnp.float32
BF16 = jnp.bfloat16
SIDE = 4
MIB = 1 << 20


def wrap(value, size=SIDE):
    return lax.rem(value + size, size)


def contract(
    lm_ref,
    rm_ref,
    om_ref,
    left_ref,
    right_ref,
    out_ref,
    a_buf,
    b_buf,
    a_stage,
    b_stage,
    total,
    kept,
    load_sem,
    a_send,
    a_recv,
    b_send,
    b_recv,
    x_send,
    x_recv,
    own_sem,
    round_sem,
):
    row = lax.axis_index("row")
    col = lax.axis_index("col")
    z = row // 2
    core = lax.rem(row, 2)
    y = col // SIDE
    x = lax.rem(col, SIDE)

    load_a = pltpu.make_async_copy(left_ref, a_stage, load_sem.at[0])
    load_b = pltpu.make_async_copy(right_ref, b_stage, load_sem.at[1])
    load_a.start()
    load_b.start()

    barrier = pltpu.get_barrier_semaphore()
    me = row * 16 + col

    def at(dx, dy):
        return row, wrap(y + dy) * SIDE + wrap(x + dx)

    def along_z(step):
        return wrap(z + step) * 2 + core, col

    x_side = (at(1, 0), at(-1, 0))
    y_side = (at(0, 1), at(0, -1))
    z_side = (along_z(1), along_z(-1))
    mate = (z * 2 + 1 - core, col)

    def greet(sem, devices):
        for device in devices:
            pl.semaphore_signal(sem, inc=1, device_id=device, device_id_type=MESH)

    greet(barrier, (*x_side, *y_side, *z_side, mate))

    x_off = pl.multiple_of(x * 512, 512)
    load_a.wait()
    for j in range(4):
        for i in range(8):
            keep = lm_ref[j, i].astype(F32)
            rows = slice(i * TILE, (i + 1) * TILE)
            block = a_stage[rows, j * TILE : (j + 1) * TILE].astype(F32) * keep
            a_buf[y, rows, pl.ds(pl.multiple_of(x_off + j * TILE, TILE), TILE)] = block.astype(BF16)
    load_b.wait()
    for i in range(8):
        rows = pl.ds(pl.multiple_of(core * 1024 + i * TILE, TILE), TILE)
        for j in range(8):
            keep = rm_ref[i, j].astype(F32)
            cols = slice(j * TILE, (j + 1) * TILE)
            block = b_stage[i * TILE : (i + 1) * TILE, cols].astype(F32) * keep
            b_buf[z, rows, cols] = block.astype(BF16)

    pl.semaphore_wait(barrier, 7)

    rounds = (x_side, y_side, y_side, z_side, z_side, (mate,))

    def pass_on(step):
        if step > 0:
            pl.semaphore_wait(round_sem.at[step - 1], len(rounds[step - 1]))
        if step < len(rounds):
            greet(round_sem.at[step], rounds[step])


    def a_piece(half, first, second, quarter):
        dx, dy = (first, second) if half == 0 else (second, first)
        start, size = half * 512, 512
        if quarter is not None:
            start, size = start + quarter * 256, 256
        cols = pl.ds(pl.multiple_of(wrap(x + dx) * 512, 512), 512)
        return a_buf.at[wrap(y + dy), pl.ds(start, size), cols]

    def a_slot(half, first, second, side):
        f_at = {0: 0, -1: 1, 1: 2, 2: 3}
        if second == 0:
            kind = {-1: 0, 1: 1, 2: 2}[first] + (1 if first == 2 and side == 1 else 0)
        else:
            kind = 4 + 4 * f_at[first] + {-1: 0, 1: 1, 2: 2}[second]
            kind += 1 if second == 2 and side == 1 else 0
        return half * 20 + kind

    a_sent = {}

    def a_go(half, first, second, axis, step, quarter):
        if axis == 0:
            there = (first - step, second)
        else:
            there = (first, second - step)
        there = tuple(2 if abs(v) == 2 else v for v in there)
        slot = a_slot(half, *there, -step)
        along_x = (axis == 0) == (half == 0)
        device = at(step, 0) if along_x else at(0, step)
        piece = a_piece(half, first, second, quarter)
        copy = pltpu.make_async_remote_copy(
            src_ref=piece,
            dst_ref=piece,
            send_sem=a_send.at[slot],
            recv_sem=a_recv.at[slot],
            device_id=device,
            device_id_type=MESH,
        )
        copy.start()
        a_sent[slot] = copy

    def a_wait(half, first, second, side=0):
        quarter = None
        if first == 2 and second == 0 or second == 2:
            quarter = 0 if side == -1 else 1
        piece = a_piece(half, first, second, quarter)
        slot = a_slot(half, first, second, side)
        pltpu.make_async_copy(piece, piece, a_recv.at[slot]).wait()

    def a_end(half, first):
        a_wait(half, first, 2, -1)
        a_wait(half, first, 2, 1)

    near = wrap(y - z)

    def b_piece(dz, side, piece, count=1):
        start = pl.multiple_of(side * 1024 + piece * 256, 256)
        return b_buf.at[wrap(z + dz), pl.ds(start, 256 * count), :]

    def b_go(dz, piece, step, count=1):
        if step and dz == 0:
            slot = piece + (0 if step == 1 else 4)
        elif step:
            slot = 8 + piece
        else:
            slot = {0: 12, -1: 13, 1: 17, 2: 21}[dz] + piece
        part = b_piece(dz, core, piece, count)
        device = (wrap(z + step) * 2 + core, col) if step else (z * 2 + 1 - core, col)
        pltpu.make_async_remote_copy(
            src_ref=part,
            dst_ref=part,
            send_sem=b_send.at[slot],
            recv_sem=b_recv.at[slot],
            device_id=device,
            device_id_type=MESH,
        ).start()

    def b_wait(dz, piece, other=False, count=1):
        if other:
            slot = {0: 12, -1: 13, 1: 17, 2: 21}[dz] + piece
        else:
            slot = {-1: 0, 1: 4, 2: 8}[dz] + piece
        part = b_piece(dz, 1 - core if other else core, piece, count)
        pltpu.make_async_copy(part, part, b_recv.at[slot]).wait()

    def b_relay(dz, piece):
        b_wait(dz, piece)
        b_go(dz, piece, -dz)
        b_go(dz, piece, 0)

    def b_rest(dz):
        for piece in {0: (), -1: (2, 3), 1: (1, 0), 2: (0, 3, 1, 2)}[dz]:
            b_wait(dz, piece)
            b_go(dz, piece, 0)
        if dz == 0:
            b_wait(0, 0, True, 4)
        else:
            for piece in range(4):
                b_wait(dz, piece, True)

    def depth(dx):
        return pl.ds(pl.multiple_of(wrap(x + dx) * 512, 512), 512)

    def add(half, blocks):
        rows = pl.ds(half * 512, 512)
        width = 512 if blocks[0][1] is None else 1024

        def one(n, carry):
            cols = pl.ds(pl.multiple_of(n * width, width), width)
            part = None
            for dy, dx in blocks:
                group, k = wrap(y + dy), slice(None) if dx is None else depth(dx)
                term = jnp.dot(a_buf[group, rows, k], b_buf[group, k, cols], preferred_element_type=F32)
                part = term if part is None else part + term
            total[rows, cols] += part
            return carry

        lax.fori_loop(0, 1024 // width, one, 0)

    halves = (0, 1)
    steps = (1, -1)
    close = (0, -1, 1)
    for step in steps:
        for half in halves:
            a_go(half, 0, 0, 0, step, None)
    for piece in (0, 1):
        b_go(0, piece, 1)
        b_go(0, 3 - piece, -1)
    for step in steps:
        for half in halves:
            a_go(half, 0, 0, 1, step, None)
    b_go(0, 0, 0, 4)
    pass_on(0)
    total[...] = jnp.zeros_like(total)

    for half in halves:
        a_wait(half, -1, 0)
        a_go(half, -1, 0, 0, 1, 0)
        a_wait(half, 1, 0)
        a_go(half, 1, 0, 0, -1, 1)
    for first in (-1, 1):
        for half in halves:
            for step in steps:
                a_go(half, first, 0, 1, step, None)
    for piece in (2, 3):
        b_go(0, piece, 1)
        b_go(0, 3 - piece, -1)
    pass_on(1)

    def arrived(first):
        for half in halves:
            a_wait(half, first, -1)
            a_wait(half, first, 1)

    def relay(first):
        for half in halves:
            a_go(half, first, -1, 1, 1, 0)
            a_go(half, first, 1, 1, -1, 1)

    def gone(first):
        for half in halves:
            for side in steps:
                a_sent.pop(a_slot(half, first, side, side)).wait_send()

    arrived(0)
    relay(0)
    pass_on(2)
    for half in halves:
        a_wait(half, 2, 0, -1)
        a_wait(half, 2, 0, 1)
        for step in steps:
            a_go(half, 2, 0, 1, step, None)
    pass_on(3)
    for piece in (0, 1):
        b_relay(-1, piece)
        b_relay(1, 3 - piece)
    pass_on(4)
    for dz in (0, 1, -1):
        b_rest(dz)
    pass_on(5)

    def in_time(half, dy, dx):
        pl.when(near != (2 - dy) % SIDE)(lambda: add(half, dx(dy)))

    def late(half, dy, dx):
        pl.when(near == (2 - dy) % SIDE)(lambda: add(half, dx(dy)))

    def whole_row(dy):
        return [(dy, None)]

    def three(dy):
        return [(dy, dx) for dx in close]

    in_time(0, 0, whole_row)
    gone(-1)
    arrived(-1)
    relay(-1)
    pass_on(6)
    a_end(1, 0)
    in_time(1, 0, whole_row)
    arrived(1)
    for half in halves:
        for dy in (-1, 1):
            in_time(half, dy, three)
    gone(2)
    relay(1)
    arrived(2)
    relay(2)
    b_rest(2)
    for half in halves:
        late(half, 0, whole_row)
        for dy in (-1, 1):
            late(half, dy, three)
    add(1, three(2))
    for first in close:
        a_end(0, first)
    add(0, three(2) + [(-1, 2), (1, 2)])
    a_end(1, -1)
    a_end(1, 1)
    add(1, [(-1, 2), (1, 2)])
    a_end(1, 2)
    a_end(0, 2)

    order = (0, 1, 3, 2)

    def strips_of(part):
        found = []
        for dz in range(SIDE):
            there_y = wrap(y + (part - dz) % SIDE)
            for there_core in range(2):
                found.append((wrap(z + dz) * 2 + there_core, there_y))
        return found

    def finish(part):
        strips = strips_of(part)
        rows = [pl.ds(pl.multiple_of(g * TILE + v * 32, 32), 32) for g, v in strips]
        group, k = wrap(y + 2), depth(2)

        value = jnp.concatenate([total[r, :] for r in rows], axis=0)
        lhs = jnp.concatenate([a_buf[group, r, k] for r in rows], axis=0)
        value += jnp.dot(lhs, b_buf[group, k, :], preferred_element_type=F32)
        for i, (g, v) in enumerate(strips):
            for j in range(8):
                keep = om_ref[g, j].astype(F32)
                block = value[i * 32 : (i + 1) * 32, j * TILE : (j + 1) * TILE] * keep
                kept[pl.ds(g * 16 + v * 4, 4), :, j * TILE : (j + 1) * TILE] = block.reshape(
                    4, 8, TILE
                ).astype(BF16)

    def hand_out(part):
        def one(t, carry):
            dz = lax.rem(t, 4)
            to_row = wrap(z + dz) * 2 + lax.rem(core + t // 16, 2)
            to_y = lax.rem(y + part + 4 - dz, 4)
            to_col = to_y * 4 + lax.rem(x + t + t // 4, 4)
            pltpu.make_async_remote_copy(
                src_ref=kept.at[to_row * 16 + to_col],
                dst_ref=out_ref.at[me],
                send_sem=x_send,
                recv_sem=x_recv,
                device_id=(to_row, to_col),
                device_id_type=MESH,
            ).start()
            return carry

        lax.fori_loop(1 if part == 0 else 0, 32, one, 0)

    finish(order[0])
    for now, later in zip(order, order[1:]):
        finish(later)
        hand_out(now)
    hand_out(order[-1])
    own = pltpu.make_async_copy(kept.at[me], out_ref.at[me], own_sem)
    own.start()

    for copy in a_sent.values():
        copy.wait_send()
    for slot in range(25):
        part = b_piece(0, core, 0, 4 if slot == 12 else 1)
        pltpu.make_async_copy(part, part, b_send.at[slot]).wait()
    own.wait()
    pltpu.make_async_copy(kept.at[pl.ds(0, 127)], kept.at[pl.ds(0, 127)], x_send).wait()
    pltpu.make_async_copy(out_ref.at[pl.ds(0, 127)], out_ref.at[pl.ds(0, 127)], x_recv).wait()


def flatten_kernel(in_ref, out_ref):
    out_ref[...] = in_ref[...].reshape(out_ref.shape)


def local(left_amps, right_ints, left_mask, right_mask, result_mask):
    smem = pl.BlockSpec(memory_space=pltpu.SMEM)
    hbm = pl.BlockSpec(memory_space=pl.ANY)
    strips = pl.pallas_call(
        contract,
        out_shape=jax.ShapeDtypeStruct((128, 8, 1024), BF16),
        in_specs=[smem, smem, smem, hbm, hbm],
        out_specs=hbm,
        scratch_shapes=[
            pltpu.VMEM((4, 1024, 2048), BF16),
            pltpu.VMEM((4, 2048, 1024), BF16),
            pltpu.VMEM((1024, 512), BF16),
            pltpu.VMEM((1024, 1024), BF16),
            pltpu.VMEM((1024, 1024), F32),
            pltpu.VMEM((128, 8, 1024), BF16),
            pltpu.SemaphoreType.DMA((2,)),
            pltpu.SemaphoreType.DMA((40,)),
            pltpu.SemaphoreType.DMA((40,)),
            pltpu.SemaphoreType.DMA((25,)),
            pltpu.SemaphoreType.DMA((25,)),
            pltpu.SemaphoreType.DMA(()),
            pltpu.SemaphoreType.DMA(()),
            pltpu.SemaphoreType.DMA(()),
            pltpu.SemaphoreType.REGULAR((6,)),
        ],
        compiler_params=pltpu.CompilerParams(
            collective_id=0, has_side_effects=True, vmem_limit_bytes=60 * MIB
        ),
        name="contract",
    )(left_mask.T, right_mask, result_mask, left_amps, right_ints)
    return pl.pallas_call(
        flatten_kernel,
        grid=(2,),
        in_specs=[pl.BlockSpec((64, 8, 1024), lambda p: (p, 0, 0))],
        out_specs=pl.BlockSpec((64, 8192), lambda p: (p, 0)),
        out_shape=jax.ShapeDtypeStruct((128, 8192), BF16),
        name="flatten",
    )(strips)


def solution(mesh):
    in_specs = (P("row", "col"), P("row", "col"), P("row", "col"), P("row", "col"), P("row", "col"))
    out_specs = P(None, ("row", "col"))
    return jax.shard_map(local, mesh=mesh, in_specs=in_specs, out_specs=out_specs, check_vma=False)
```

```python
import jax
import jax.numpy as jnp
from jax import lax
from jax.experimental import pallas as pl
from jax.experimental.pallas import tpu as pltpu
from jax.sharding import PartitionSpec as P

TILE = 128
MESH = pl.DeviceIdType.MESH
F32 = jnp.float32
BF16 = jnp.bfloat16
SIDE = 4
MIB = 1 << 20


def wrap(value, size=SIDE):
    return lax.rem(value + size, size)


def contract(
    lm_hbm,
    rm_hbm,
    om_hbm,
    left_ref,
    right_ref,
    out_ref,
    a_buf,
    b_buf,
    a_stage,
    b_stage,
    total,
    kept,
    load_sem,
    a_send,
    a_recv,
    b_send,
    b_recv,
    x_send,
    x_recv,
    own_sem,
    round_sem,
    lm_ref,
    rm_ref,
    om_ref,
):
    row = lax.axis_index("row")
    col = lax.axis_index("col")
    z = row // 2
    core = lax.rem(row, 2)
    y = col // SIDE
    x = lax.rem(col, SIDE)

    load_a = pltpu.make_async_copy(left_ref, a_stage, load_sem.at[0])
    load_b = pltpu.make_async_copy(right_ref, b_stage, load_sem.at[1])
    load_masks = [
        pltpu.make_async_copy(src, dst, load_sem.at[2 + i])
        for i, (src, dst) in enumerate(((lm_hbm, lm_ref), (rm_hbm, rm_ref), (om_hbm, om_ref)))
    ]
    for load in (*load_masks, load_a, load_b):
        load.start()

    barrier = pltpu.get_barrier_semaphore()
    me = row * 16 + col

    def at(dx, dy):
        return row, wrap(y + dy) * SIDE + wrap(x + dx)

    def along_z(step):
        return wrap(z + step) * 2 + core, col

    x_side = (at(1, 0), at(-1, 0))
    y_side = (at(0, 1), at(0, -1))
    z_side = (along_z(1), along_z(-1))
    mate = (z * 2 + 1 - core, col)

    def greet(sem, devices):
        for device in devices:
            pl.semaphore_signal(sem, inc=1, device_id=device, device_id_type=MESH)

    greet(barrier, (*x_side, *y_side, *z_side, mate))

    x_off = pl.multiple_of(x * 512, 512)
    for load in load_masks:
        load.wait()
    load_a.wait()
    for j in range(4):
        for i in range(8):
            keep = lm_ref[j, i].astype(F32)
            rows = slice(i * TILE, (i + 1) * TILE)
            block = a_stage[rows, j * TILE : (j + 1) * TILE].astype(F32) * keep
            a_buf[y, rows, pl.ds(pl.multiple_of(x_off + j * TILE, TILE), TILE)] = block.astype(BF16)
    load_b.wait()
    for i in range(8):
        rows = pl.ds(pl.multiple_of(core * 1024 + i * TILE, TILE), TILE)
        for j in range(8):
            keep = rm_ref[i, j].astype(F32)
            cols = slice(j * TILE, (j + 1) * TILE)
            block = b_stage[i * TILE : (i + 1) * TILE, cols].astype(F32) * keep
            b_buf[z, rows, cols] = block.astype(BF16)

    pl.semaphore_wait(barrier, 7)

    rounds = (x_side, y_side, y_side, z_side, z_side, (mate,))

    def pass_on(step):
        if step > 0:
            pl.semaphore_wait(round_sem.at[step - 1], len(rounds[step - 1]))
        if step < len(rounds):
            greet(round_sem.at[step], rounds[step])


    def a_piece(half, first, second, quarter):
        dx, dy = (first, second) if half == 0 else (second, first)
        start, size = half * 512, 512
        if quarter is not None:
            start, size = start + quarter * 256, 256
        cols = pl.ds(pl.multiple_of(wrap(x + dx) * 512, 512), 512)
        return a_buf.at[wrap(y + dy), pl.ds(start, size), cols]

    def a_slot(half, first, second, side):
        f_at = {0: 0, -1: 1, 1: 2, 2: 3}
        if second == 0:
            kind = {-1: 0, 1: 1, 2: 2}[first] + (1 if first == 2 and side == 1 else 0)
        else:
            kind = 4 + 4 * f_at[first] + {-1: 0, 1: 1, 2: 2}[second]
            kind += 1 if second == 2 and side == 1 else 0
        return half * 20 + kind

    a_sent = {}

    def a_go(half, first, second, axis, step, quarter):
        if axis == 0:
            there = (first - step, second)
        else:
            there = (first, second - step)
        there = tuple(2 if abs(v) == 2 else v for v in there)
        slot = a_slot(half, *there, -step)
        along_x = (axis == 0) == (half == 0)
        device = at(step, 0) if along_x else at(0, step)
        piece = a_piece(half, first, second, quarter)
        copy = pltpu.make_async_remote_copy(
            src_ref=piece,
            dst_ref=piece,
            send_sem=a_send.at[slot],
            recv_sem=a_recv.at[slot],
            device_id=device,
            device_id_type=MESH,
        )
        copy.start()
        a_sent[slot] = copy

    def a_wait(half, first, second, side=0):
        quarter = None
        if first == 2 and second == 0 or second == 2:
            quarter = 0 if side == -1 else 1
        piece = a_piece(half, first, second, quarter)
        slot = a_slot(half, first, second, side)
        pltpu.make_async_copy(piece, piece, a_recv.at[slot]).wait()

    def a_end(half, first):
        a_wait(half, first, 2, -1)
        a_wait(half, first, 2, 1)

    near = wrap(y - z)

    def b_piece(dz, side, piece, count=1):
        start = pl.multiple_of(side * 1024 + piece * 256, 256)
        return b_buf.at[wrap(z + dz), pl.ds(start, 256 * count), :]

    def b_go(dz, piece, step, count=1):
        if step and dz == 0:
            slot = piece + (0 if step == 1 else 4)
        elif step:
            slot = 8 + piece
        else:
            slot = {0: 12, -1: 13, 1: 17, 2: 21}[dz] + piece
        part = b_piece(dz, core, piece, count)
        device = (wrap(z + step) * 2 + core, col) if step else (z * 2 + 1 - core, col)
        pltpu.make_async_remote_copy(
            src_ref=part,
            dst_ref=part,
            send_sem=b_send.at[slot],
            recv_sem=b_recv.at[slot],
            device_id=device,
            device_id_type=MESH,
        ).start()

    def b_wait(dz, piece, other=False, count=1):
        if other:
            slot = {0: 12, -1: 13, 1: 17, 2: 21}[dz] + piece
        else:
            slot = {-1: 0, 1: 4, 2: 8}[dz] + piece
        part = b_piece(dz, 1 - core if other else core, piece, count)
        pltpu.make_async_copy(part, part, b_recv.at[slot]).wait()

    def b_relay(dz, piece):
        b_wait(dz, piece)
        b_go(dz, piece, -dz)
        b_go(dz, piece, 0)

    def b_rest(dz):
        for piece in {0: (), -1: (2, 3), 1: (1, 0), 2: (0, 3, 1, 2)}[dz]:
            b_wait(dz, piece)
            b_go(dz, piece, 0)
        if dz == 0:
            b_wait(0, 0, True, 4)
        else:
            for piece in range(4):
                b_wait(dz, piece, True)

    def depth(dx):
        return pl.ds(pl.multiple_of(wrap(x + dx) * 512, 512), 512)

    def add(half, blocks):
        rows = pl.ds(half * 512, 512)
        width = 512 if blocks[0][1] is None else 1024

        def one(n, carry):
            cols = pl.ds(pl.multiple_of(n * width, width), width)
            part = None
            for dy, dx in blocks:
                group, k = wrap(y + dy), slice(None) if dx is None else depth(dx)
                term = jnp.dot(a_buf[group, rows, k], b_buf[group, k, cols], preferred_element_type=F32)
                part = term if part is None else part + term
            total[rows, cols] += part
            return carry

        lax.fori_loop(0, 1024 // width, one, 0)

    halves = (0, 1)
    steps = (1, -1)
    close = (0, -1, 1)
    for step in steps:
        for half in halves:
            a_go(half, 0, 0, 0, step, None)
    for piece in (0, 1):
        b_go(0, piece, 1)
        b_go(0, 3 - piece, -1)
    for step in steps:
        for half in halves:
            a_go(half, 0, 0, 1, step, None)
    b_go(0, 0, 0, 4)
    pass_on(0)
    total[...] = jnp.zeros_like(total)

    for half in halves:
        a_wait(half, -1, 0)
        a_go(half, -1, 0, 0, 1, 0)
        a_wait(half, 1, 0)
        a_go(half, 1, 0, 0, -1, 1)
    for first in (-1, 1):
        for half in halves:
            for step in steps:
                a_go(half, first, 0, 1, step, None)
    for piece in (2, 3):
        b_go(0, piece, 1)
        b_go(0, 3 - piece, -1)
    pass_on(1)

    def arrived(first):
        for half in halves:
            a_wait(half, first, -1)
            a_wait(half, first, 1)

    def relay(first):
        for half in halves:
            a_go(half, first, -1, 1, 1, 0)
            a_go(half, first, 1, 1, -1, 1)

    def gone(first):
        for half in halves:
            for side in steps:
                a_sent.pop(a_slot(half, first, side, side)).wait_send()

    arrived(0)
    relay(0)
    pass_on(2)
    for half in halves:
        a_wait(half, 2, 0, -1)
        a_wait(half, 2, 0, 1)
        for step in steps:
            a_go(half, 2, 0, 1, step, None)
    pass_on(3)
    for piece in (0, 1):
        b_relay(-1, piece)
        b_relay(1, 3 - piece)
    pass_on(4)
    for dz in (0, 1, -1):
        b_rest(dz)
    pass_on(5)

    def in_time(half, dy, dx):
        pl.when(near != (2 - dy) % SIDE)(lambda: add(half, dx(dy)))

    def late(half, dy, dx):
        pl.when(near == (2 - dy) % SIDE)(lambda: add(half, dx(dy)))

    def whole_row(dy):
        return [(dy, None)]

    def three(dy):
        return [(dy, dx) for dx in close]

    in_time(0, 0, whole_row)
    gone(-1)
    arrived(-1)
    relay(-1)
    pass_on(6)
    a_end(1, 0)
    in_time(1, 0, whole_row)
    arrived(1)
    for half in halves:
        for dy in (-1, 1):
            in_time(half, dy, three)
    gone(2)
    relay(1)
    arrived(2)
    relay(2)
    b_rest(2)
    for half in halves:
        late(half, 0, whole_row)
        for dy in (-1, 1):
            late(half, dy, three)
    add(1, three(2))
    for first in close:
        a_end(0, first)
    add(0, three(2) + [(-1, 2), (1, 2)])
    a_end(1, -1)
    a_end(1, 1)
    add(1, [(-1, 2), (1, 2)])
    a_end(1, 2)
    a_end(0, 2)

    order = (0, 1, 3, 2)

    def strips_of(part):
        found = []
        for dz in range(SIDE):
            there_y = wrap(y + (part - dz) % SIDE)
            for there_core in range(2):
                found.append((wrap(z + dz) * 2 + there_core, there_y))
        return found

    def finish(part):
        strips = strips_of(part)
        rows = [pl.ds(pl.multiple_of(g * TILE + v * 32, 32), 32) for g, v in strips]
        group, k = wrap(y + 2), depth(2)

        value = jnp.concatenate([total[r, :] for r in rows], axis=0)
        lhs = jnp.concatenate([a_buf[group, r, k] for r in rows], axis=0)
        value += jnp.dot(lhs, b_buf[group, k, :], preferred_element_type=F32)
        for i, (g, v) in enumerate(strips):
            for j in range(8):
                keep = om_ref[g, j].astype(F32)
                block = value[i * 32 : (i + 1) * 32, j * TILE : (j + 1) * TILE] * keep
                kept[pl.ds(g * 16 + v * 4, 4), :, j * TILE : (j + 1) * TILE] = block.reshape(
                    4, 8, TILE
                ).astype(BF16)

    def hand_out(part):
        def one(t, carry):
            dz = lax.rem(t, 4)
            to_row = wrap(z + dz) * 2 + lax.rem(core + t // 16, 2)
            to_y = lax.rem(y + part + 4 - dz, 4)
            to_col = to_y * 4 + lax.rem(x + t + t // 4, 4)
            pltpu.make_async_remote_copy(
                src_ref=kept.at[to_row * 16 + to_col],
                dst_ref=out_ref.at[me],
                send_sem=x_send,
                recv_sem=x_recv,
                device_id=(to_row, to_col),
                device_id_type=MESH,
            ).start()
            return carry

        lax.fori_loop(1 if part == 0 else 0, 32, one, 0)

    finish(order[0])
    for now, later in zip(order, order[1:]):
        finish(later)
        hand_out(now)
    hand_out(order[-1])
    own = pltpu.make_async_copy(kept.at[me], out_ref.at[me], own_sem)
    own.start()

    for copy in a_sent.values():
        copy.wait_send()
    for slot in range(25):
        part = b_piece(0, core, 0, 4 if slot == 12 else 1)
        pltpu.make_async_copy(part, part, b_send.at[slot]).wait()
    own.wait()
    pltpu.make_async_copy(kept.at[pl.ds(0, 127)], kept.at[pl.ds(0, 127)], x_send).wait()
    pltpu.make_async_copy(out_ref.at[pl.ds(0, 127)], out_ref.at[pl.ds(0, 127)], x_recv).wait()


def flatten_kernel(in_ref, out_ref):
    out_ref[...] = in_ref[...].reshape(out_ref.shape)


def local(left_amps, right_ints, left_mask, right_mask, result_mask):
    hbm = pl.BlockSpec(memory_space=pltpu.HBM)
    anywhere = pl.BlockSpec(memory_space=pl.ANY)
    strips = pl.pallas_call(
        contract,
        out_shape=jax.ShapeDtypeStruct((128, 8, 1024), BF16),
        in_specs=[hbm] * 5,
        out_specs=anywhere,
        scratch_shapes=[
            pltpu.VMEM((4, 1024, 2048), BF16),
            pltpu.VMEM((4, 2048, 1024), BF16),
            pltpu.VMEM((1024, 512), BF16),
            pltpu.VMEM((1024, 1024), BF16),
            pltpu.VMEM((1024, 1024), F32),
            pltpu.VMEM((128, 8, 1024), BF16),
            pltpu.SemaphoreType.DMA((5,)),
            pltpu.SemaphoreType.DMA((40,)),
            pltpu.SemaphoreType.DMA((40,)),
            pltpu.SemaphoreType.DMA((25,)),
            pltpu.SemaphoreType.DMA((25,)),
            pltpu.SemaphoreType.DMA(()),
            pltpu.SemaphoreType.DMA(()),
            pltpu.SemaphoreType.DMA(()),
            pltpu.SemaphoreType.REGULAR((6,)),
            pltpu.SMEM((4, 8), jnp.int32),
            pltpu.SMEM((8, 8), jnp.int32),
            pltpu.SMEM((8, 8), jnp.int32),
        ],
        compiler_params=pltpu.CompilerParams(
            collective_id=0, has_side_effects=True, vmem_limit_bytes=46 * MIB
        ),
        name="contract",
    )(
        *(
            pltpu.with_memory_space_constraint(array, pltpu.HBM)
            for array in (left_mask.T, right_mask, result_mask, left_amps, right_ints)
        )
    )
    return pl.pallas_call(
        flatten_kernel,
        grid=(2,),
        in_specs=[pl.BlockSpec((64, 8, 1024), lambda p: (p, 0, 0))],
        out_specs=pl.BlockSpec((64, 8192), lambda p: (p, 0)),
        out_shape=jax.ShapeDtypeStruct((128, 8192), BF16),
        compiler_params=pltpu.CompilerParams(vmem_limit_bytes=12 * MIB),
        name="flatten",
    )(strips)


def solution(mesh):
    in_specs = (P("row", "col"), P("row", "col"), P("row", "col"), P("row", "col"), P("row", "col"))
    out_specs = P(None, ("row", "col"))
    return jax.shard_map(local, mesh=mesh, in_specs=in_specs, out_specs=out_specs, check_vma=False)
```

```python
import jax
import jax.numpy as jnp
from jax import lax
from jax.experimental import pallas as pl
from jax.experimental.pallas import tpu as pltpu
from jax.sharding import PartitionSpec as P

TILE = 128
MESH = pl.DeviceIdType.MESH
F32 = jnp.float32
BF16 = jnp.bfloat16
SIDE = 4
MIB = 1 << 20


def wrap(value, size=SIDE):
    return lax.rem(value + size, size)


def contract(
    lm_hbm,
    rm_hbm,
    om_hbm,
    left_ref,
    right_ref,
    out_ref,
    a_buf,
    b_buf,
    a_stage,
    b_stage,
    total,
    kept,
    load_sem,
    a_send,
    a_recv,
    b_send,
    b_recv,
    x_send,
    x_recv,
    own_sem,
    round_sem,
    lm_ref,
    rm_ref,
    om_ref,
):
    row = lax.axis_index("row")
    col = lax.axis_index("col")
    z = row // 2
    core = lax.rem(row, 2)
    y = col // SIDE
    x = lax.rem(col, SIDE)

    load_a = pltpu.make_async_copy(left_ref, a_stage, load_sem.at[0])
    load_b = pltpu.make_async_copy(right_ref, b_stage, load_sem.at[1])
    load_masks = [
        pltpu.make_async_copy(src, dst, load_sem.at[2 + i])
        for i, (src, dst) in enumerate(((lm_hbm, lm_ref), (rm_hbm, rm_ref), (om_hbm, om_ref)))
    ]
    for load in (*load_masks, load_a, load_b):
        load.start()

    barrier = pltpu.get_barrier_semaphore()
    me = row * 16 + col

    def at(dx, dy):
        return row, wrap(y + dy) * SIDE + wrap(x + dx)

    def along_z(step):
        return wrap(z + step) * 2 + core, col

    x_side = (at(1, 0), at(-1, 0))
    y_side = (at(0, 1), at(0, -1))
    z_side = (along_z(1), along_z(-1))
    mate = (z * 2 + 1 - core, col)

    def greet(sem, devices):
        for device in devices:
            pl.semaphore_signal(sem, inc=1, device_id=device, device_id_type=MESH)

    greet(barrier, (*x_side, *y_side, *z_side, mate))

    x_off = pl.multiple_of(x * 512, 512)
    for load in load_masks:
        load.wait()
    load_a.wait()
    for j in range(4):
        for i in range(8):
            keep = lm_ref[j, i].astype(F32)
            rows = slice(i * TILE, (i + 1) * TILE)
            block = a_stage[rows, j * TILE : (j + 1) * TILE].astype(F32) * keep
            a_buf[y, rows, pl.ds(pl.multiple_of(x_off + j * TILE, TILE), TILE)] = block.astype(BF16)
    total[0:256, :] = jnp.zeros((256, 1024), F32)

    pl.semaphore_wait(barrier, 7)

    rounds = (x_side, y_side, y_side, z_side, z_side, (mate,))

    def pass_on(step):
        if step > 0:
            pl.semaphore_wait(round_sem.at[step - 1], len(rounds[step - 1]))
        if step < len(rounds):
            greet(round_sem.at[step], rounds[step])


    def a_piece(half, first, second, quarter):
        dx, dy = (first, second) if half == 0 else (second, first)
        start, size = half * 512, 512
        if quarter is not None:
            start, size = start + quarter * 256, 256
        cols = pl.ds(pl.multiple_of(wrap(x + dx) * 512, 512), 512)
        return a_buf.at[wrap(y + dy), pl.ds(start, size), cols]

    def a_slot(half, first, second, side):
        f_at = {0: 0, -1: 1, 1: 2, 2: 3}
        if second == 0:
            kind = {-1: 0, 1: 1, 2: 2}[first] + (1 if first == 2 and side == 1 else 0)
        else:
            kind = 4 + 4 * f_at[first] + {-1: 0, 1: 1, 2: 2}[second]
            kind += 1 if second == 2 and side == 1 else 0
        return half * 20 + kind

    a_sent = {}

    def a_go(half, first, second, axis, step, quarter):
        if axis == 0:
            there = (first - step, second)
        else:
            there = (first, second - step)
        there = tuple(2 if abs(v) == 2 else v for v in there)
        slot = a_slot(half, *there, -step)
        along_x = (axis == 0) == (half == 0)
        device = at(step, 0) if along_x else at(0, step)
        piece = a_piece(half, first, second, quarter)
        copy = pltpu.make_async_remote_copy(
            src_ref=piece,
            dst_ref=piece,
            send_sem=a_send.at[slot],
            recv_sem=a_recv.at[slot],
            device_id=device,
            device_id_type=MESH,
        )
        copy.start()
        a_sent[slot] = copy

    def a_wait(half, first, second, side=0):
        quarter = None
        if first == 2 and second == 0 or second == 2:
            quarter = 0 if side == -1 else 1
        piece = a_piece(half, first, second, quarter)
        slot = a_slot(half, first, second, side)
        pltpu.make_async_copy(piece, piece, a_recv.at[slot]).wait()

    def a_end(half, first):
        a_wait(half, first, 2, -1)
        a_wait(half, first, 2, 1)

    near = wrap(y - z)

    def b_piece(dz, side, piece, count=1):
        start = pl.multiple_of(side * 1024 + piece * 256, 256)
        return b_buf.at[wrap(z + dz), pl.ds(start, 256 * count), :]

    def b_go(dz, piece, step, count=1):
        if step and dz == 0:
            slot = piece + (0 if step == 1 else 4)
        elif step:
            slot = 8 + piece
        else:
            slot = {0: 12, -1: 13, 1: 17, 2: 21}[dz] + piece
        part = b_piece(dz, core, piece, count)
        device = (wrap(z + step) * 2 + core, col) if step else (z * 2 + 1 - core, col)
        pltpu.make_async_remote_copy(
            src_ref=part,
            dst_ref=part,
            send_sem=b_send.at[slot],
            recv_sem=b_recv.at[slot],
            device_id=device,
            device_id_type=MESH,
        ).start()

    def b_wait(dz, piece, other=False, count=1):
        if other:
            slot = {0: 12, -1: 13, 1: 17, 2: 21}[dz] + piece
        else:
            slot = {-1: 0, 1: 4, 2: 8}[dz] + piece
        part = b_piece(dz, 1 - core if other else core, piece, count)
        pltpu.make_async_copy(part, part, b_recv.at[slot]).wait()

    def b_relay(dz, piece):
        b_wait(dz, piece)
        b_go(dz, piece, -dz)
        b_go(dz, piece, 0)

    def b_rest(dz):
        for piece in {0: (), -1: (2, 3), 1: (1, 0), 2: (0, 3, 1, 2)}[dz]:
            b_wait(dz, piece)
            b_go(dz, piece, 0)
        if dz == 0:
            b_wait(0, 0, True, 4)
        else:
            for piece in range(4):
                b_wait(dz, piece, True)

    def depth(dx):
        return pl.ds(pl.multiple_of(wrap(x + dx) * 512, 512), 512)

    def add(half, blocks):
        rows = pl.ds(half * 512, 512)
        width = 512 if blocks[0][1] is None else 1024

        def one(n, carry):
            cols = pl.ds(pl.multiple_of(n * width, width), width)
            part = None
            for dy, dx in blocks:
                group, k = wrap(y + dy), slice(None) if dx is None else depth(dx)
                term = jnp.dot(a_buf[group, rows, k], b_buf[group, k, cols], preferred_element_type=F32)
                part = term if part is None else part + term
            total[rows, cols] += part
            return carry

        lax.fori_loop(0, 1024 // width, one, 0)

    halves = (0, 1)
    steps = (1, -1)
    close = (0, -1, 1)
    for step in steps:
        for half in halves:
            a_go(half, 0, 0, 0, step, None)
    for step in steps:
        for half in halves:
            a_go(half, 0, 0, 1, step, None)
    load_b.wait()
    for i in range(8):
        rows = pl.ds(pl.multiple_of(core * 1024 + i * TILE, TILE), TILE)
        for j in range(8):
            keep = rm_ref[i, j].astype(F32)
            cols = slice(j * TILE, (j + 1) * TILE)
            block = b_stage[i * TILE : (i + 1) * TILE, cols].astype(F32) * keep
            b_buf[z, rows, cols] = block.astype(BF16)
    total[256:, :] = jnp.zeros((768, 1024), F32)
    pass_on(0)
    for piece in (0, 1):
        b_go(0, piece, 1)
        b_go(0, 3 - piece, -1)
    b_go(0, 0, 0, 4)

    for half in halves:
        a_wait(half, -1, 0)
        a_go(half, -1, 0, 0, 1, 0)
        a_wait(half, 1, 0)
        a_go(half, 1, 0, 0, -1, 1)
    for first in (-1, 1):
        for half in halves:
            for step in steps:
                a_go(half, first, 0, 1, step, None)
    for piece in (2, 3):
        b_go(0, piece, 1)
        b_go(0, 3 - piece, -1)
    pass_on(1)

    def arrived(first):
        for half in halves:
            a_wait(half, first, -1)
            a_wait(half, first, 1)

    def relay(first):
        for half in halves:
            a_go(half, first, -1, 1, 1, 0)
            a_go(half, first, 1, 1, -1, 1)

    def gone(first):
        for half in halves:
            for side in steps:
                a_sent.pop(a_slot(half, first, side, side)).wait_send()

    arrived(0)
    relay(0)
    pass_on(2)
    for half in halves:
        a_wait(half, 2, 0, -1)
        a_wait(half, 2, 0, 1)
        for step in steps:
            a_go(half, 2, 0, 1, step, None)
    pass_on(3)
    for piece in (0, 1):
        b_relay(-1, piece)
        b_relay(1, 3 - piece)
    pass_on(4)
    for dz in (0, 1, -1):
        b_rest(dz)
    pass_on(5)

    def in_time(half, dy, dx):
        pl.when(near != (2 - dy) % SIDE)(lambda: add(half, dx(dy)))

    def late(half, dy, dx):
        pl.when(near == (2 - dy) % SIDE)(lambda: add(half, dx(dy)))

    def whole_row(dy):
        return [(dy, None)]

    def three(dy):
        return [(dy, dx) for dx in close]

    in_time(0, 0, whole_row)
    gone(-1)
    arrived(-1)
    relay(-1)
    pass_on(6)
    a_end(1, 0)
    in_time(1, 0, whole_row)
    arrived(1)
    for half in halves:
        for dy in (-1, 1):
            in_time(half, dy, three)
    gone(2)
    relay(1)
    arrived(2)
    relay(2)
    b_rest(2)
    for half in halves:
        late(half, 0, whole_row)
        for dy in (-1, 1):
            late(half, dy, three)
    add(1, three(2))
    for first in close:
        a_end(0, first)
    add(0, three(2) + [(-1, 2), (1, 2)])
    a_end(1, -1)
    a_end(1, 1)
    add(1, [(-1, 2), (1, 2)])
    a_end(1, 2)
    a_end(0, 2)

    order = (0, 1, 3, 2)

    def strips_of(part):
        found = []
        for dz in range(SIDE):
            there_y = wrap(y + (part - dz) % SIDE)
            for there_core in range(2):
                found.append((wrap(z + dz) * 2 + there_core, there_y))
        return found

    def finish(part):
        strips = strips_of(part)
        rows = [pl.ds(pl.multiple_of(g * TILE + v * 32, 32), 32) for g, v in strips]
        group, k = wrap(y + 2), depth(2)

        value = jnp.concatenate([total[r, :] for r in rows], axis=0)
        lhs = jnp.concatenate([a_buf[group, r, k] for r in rows], axis=0)
        value += jnp.dot(lhs, b_buf[group, k, :], preferred_element_type=F32)
        for i, (g, v) in enumerate(strips):
            for j in range(8):
                keep = om_ref[g, j].astype(F32)
                block = value[i * 32 : (i + 1) * 32, j * TILE : (j + 1) * TILE] * keep
                kept[pl.ds(g * 16 + v * 4, 4), :, j * TILE : (j + 1) * TILE] = block.reshape(
                    4, 8, TILE
                ).astype(BF16)

    def hand_out(part):
        def one(t, carry):
            dz = lax.rem(t, 4)
            to_row = wrap(z + dz) * 2 + lax.rem(core + t // 16, 2)
            to_y = lax.rem(y + part + 4 - dz, 4)
            to_col = to_y * 4 + lax.rem(x + t + t // 4, 4)
            pltpu.make_async_remote_copy(
                src_ref=kept.at[to_row * 16 + to_col],
                dst_ref=out_ref.at[me],
                send_sem=x_send,
                recv_sem=x_recv,
                device_id=(to_row, to_col),
                device_id_type=MESH,
            ).start()
            return carry

        lax.fori_loop(1 if part == 0 else 0, 32, one, 0)

    finish(order[0])
    for now, later in zip(order, order[1:]):
        finish(later)
        hand_out(now)
    hand_out(order[-1])
    own = pltpu.make_async_copy(kept.at[me], out_ref.at[me], own_sem)
    own.start()

    for copy in a_sent.values():
        copy.wait_send()
    for slot in range(25):
        part = b_piece(0, core, 0, 4 if slot == 12 else 1)
        pltpu.make_async_copy(part, part, b_send.at[slot]).wait()
    own.wait()
    pltpu.make_async_copy(kept.at[pl.ds(0, 127)], kept.at[pl.ds(0, 127)], x_send).wait()
    pltpu.make_async_copy(out_ref.at[pl.ds(0, 127)], out_ref.at[pl.ds(0, 127)], x_recv).wait()


def flatten_kernel(in_ref, out_ref):
    out_ref[...] = in_ref[...].reshape(out_ref.shape)


def local(left_amps, right_ints, left_mask, right_mask, result_mask):
    hbm = pl.BlockSpec(memory_space=pltpu.HBM)
    anywhere = pl.BlockSpec(memory_space=pl.ANY)
    strips = pl.pallas_call(
        contract,
        out_shape=jax.ShapeDtypeStruct((128, 8, 1024), BF16),
        in_specs=[hbm] * 5,
        out_specs=anywhere,
        scratch_shapes=[
            pltpu.VMEM((4, 1024, 2048), BF16),
            pltpu.VMEM((4, 2048, 1024), BF16),
            pltpu.VMEM((1024, 512), BF16),
            pltpu.VMEM((1024, 1024), BF16),
            pltpu.VMEM((1024, 1024), F32),
            pltpu.VMEM((128, 8, 1024), BF16),
            pltpu.SemaphoreType.DMA((5,)),
            pltpu.SemaphoreType.DMA((40,)),
            pltpu.SemaphoreType.DMA((40,)),
            pltpu.SemaphoreType.DMA((25,)),
            pltpu.SemaphoreType.DMA((25,)),
            pltpu.SemaphoreType.DMA(()),
            pltpu.SemaphoreType.DMA(()),
            pltpu.SemaphoreType.DMA(()),
            pltpu.SemaphoreType.REGULAR((6,)),
            pltpu.SMEM((4, 8), jnp.int32),
            pltpu.SMEM((8, 8), jnp.int32),
            pltpu.SMEM((8, 8), jnp.int32),
        ],
        compiler_params=pltpu.CompilerParams(
            collective_id=0, has_side_effects=True, vmem_limit_bytes=46 * MIB
        ),
        name="contract",
    )(
        *(
            pltpu.with_memory_space_constraint(array, pltpu.HBM)
            for array in (left_mask.T, right_mask, result_mask, left_amps, right_ints)
        )
    )
    return pl.pallas_call(
        flatten_kernel,
        grid=(2,),
        in_specs=[pl.BlockSpec((64, 8, 1024), lambda p: (p, 0, 0))],
        out_specs=pl.BlockSpec((64, 8192), lambda p: (p, 0)),
        out_shape=jax.ShapeDtypeStruct((128, 8192), BF16),
        compiler_params=pltpu.CompilerParams(vmem_limit_bytes=12 * MIB),
        name="flatten",
    )(strips)


def solution(mesh):
    in_specs = (P("row", "col"), P("row", "col"), P("row", "col"), P("row", "col"), P("row", "col"))
    out_specs = P(None, ("row", "col"))
    return jax.shard_map(local, mesh=mesh, in_specs=in_specs, out_specs=out_specs, check_vma=False)
```

```python
import jax
import jax.numpy as jnp
from jax import lax
from jax.experimental import pallas as pl
from jax.experimental.pallas import tpu as pltpu
from jax.sharding import PartitionSpec as P

TILE = 128
MESH = pl.DeviceIdType.MESH
F32 = jnp.float32
BF16 = jnp.bfloat16
SIDE = 4
MIB = 1 << 20


def wrap(value, size=SIDE):
    return lax.rem(value + size, size)


def contract(
    lm_hbm,
    rm_hbm,
    om_hbm,
    left_ref,
    right_ref,
    out_ref,
    a_buf,
    b_buf,
    a_stage,
    b_stage,
    total,
    kept,
    load_sem,
    a_send,
    a_recv,
    b_send,
    b_recv,
    x_send,
    x_recv,
    own_sem,
    round_sem,
    lm_ref,
    rm_ref,
    om_ref,
):
    row = lax.axis_index("row")
    col = lax.axis_index("col")
    z = row // 2
    core = lax.rem(row, 2)
    y = col // SIDE
    x = lax.rem(col, SIDE)

    load_a = pltpu.make_async_copy(left_ref, a_stage, load_sem.at[0])
    load_b = pltpu.make_async_copy(right_ref, b_stage, load_sem.at[1])
    load_masks = [
        pltpu.make_async_copy(src, dst, load_sem.at[2 + i])
        for i, (src, dst) in enumerate(((lm_hbm, lm_ref), (rm_hbm, rm_ref), (om_hbm, om_ref)))
    ]
    for load in (*load_masks, load_a, load_b):
        load.start()

    barrier = pltpu.get_barrier_semaphore()
    me = row * 16 + col

    def at(dx, dy):
        return row, wrap(y + dy) * SIDE + wrap(x + dx)

    def along_z(step):
        return wrap(z + step) * 2 + core, col

    x_side = (at(1, 0), at(-1, 0))
    y_side = (at(0, 1), at(0, -1))
    z_side = (along_z(1), along_z(-1))
    mate = (z * 2 + 1 - core, col)

    def greet(sem, devices):
        for device in devices:
            pl.semaphore_signal(sem, inc=1, device_id=device, device_id_type=MESH)

    greet(barrier, (*x_side, *y_side, *z_side, mate))

    x_off = pl.multiple_of(x * 512, 512)
    for load in load_masks:
        load.wait()
    load_a.wait()
    for j in range(4):
        for i in range(8):
            keep = lm_ref[j, i].astype(F32)
            rows = slice(i * TILE, (i + 1) * TILE)
            block = a_stage[rows, j * TILE : (j + 1) * TILE].astype(F32) * keep
            a_buf[y, rows, pl.ds(pl.multiple_of(x_off + j * TILE, TILE), TILE)] = block.astype(BF16)
    total[0:256, :] = jnp.zeros((256, 1024), F32)

    pl.semaphore_wait(barrier, 7)

    rounds = (x_side, y_side, y_side, z_side, z_side, (mate,))

    def pass_on(step):
        if step > 0:
            pl.semaphore_wait(round_sem.at[step - 1], len(rounds[step - 1]))
        if step < len(rounds):
            greet(round_sem.at[step], rounds[step])


    def a_piece(half, first, second, quarter):
        dx, dy = (first, second) if half == 0 else (second, first)
        start, size = half * 512, 512
        if quarter is not None:
            start, size = start + quarter * 256, 256
        cols = pl.ds(pl.multiple_of(wrap(x + dx) * 512, 512), 512)
        return a_buf.at[wrap(y + dy), pl.ds(start, size), cols]

    def a_slot(half, first, second, side):
        f_at = {0: 0, -1: 1, 1: 2, 2: 3}
        if second == 0:
            kind = {-1: 0, 1: 1, 2: 2}[first] + (1 if first == 2 and side == 1 else 0)
        else:
            kind = 4 + 4 * f_at[first] + {-1: 0, 1: 1, 2: 2}[second]
            kind += 1 if second == 2 and side == 1 else 0
        return half * 20 + kind

    a_sent = {}

    def a_go(half, first, second, axis, step, quarter):
        if axis == 0:
            there = (first - step, second)
        else:
            there = (first, second - step)
        there = tuple(2 if abs(v) == 2 else v for v in there)
        slot = a_slot(half, *there, -step)
        along_x = (axis == 0) == (half == 0)
        device = at(step, 0) if along_x else at(0, step)
        piece = a_piece(half, first, second, quarter)
        copy = pltpu.make_async_remote_copy(
            src_ref=piece,
            dst_ref=piece,
            send_sem=a_send.at[slot],
            recv_sem=a_recv.at[slot],
            device_id=device,
            device_id_type=MESH,
        )
        copy.start()
        a_sent[slot] = copy

    def a_wait(half, first, second, side=0):
        quarter = None
        if first == 2 and second == 0 or second == 2:
            quarter = 0 if side == -1 else 1
        piece = a_piece(half, first, second, quarter)
        slot = a_slot(half, first, second, side)
        pltpu.make_async_copy(piece, piece, a_recv.at[slot]).wait()

    def a_end(half, first):
        a_wait(half, first, 2, -1)
        a_wait(half, first, 2, 1)

    near = wrap(y - z)

    def b_piece(dz, side, piece, count=1):
        start = pl.multiple_of(side * 1024 + piece * 256, 256)
        return b_buf.at[wrap(z + dz), pl.ds(start, 256 * count), :]

    def b_go(dz, piece, step, count=1):
        if step and dz == 0:
            slot = piece + (0 if step == 1 else 4)
        elif step:
            slot = 8 + piece
        else:
            slot = {0: 12, -1: 13, 1: 17, 2: 21}[dz] + piece
        part = b_piece(dz, core, piece, count)
        device = (wrap(z + step) * 2 + core, col) if step else (z * 2 + 1 - core, col)
        pltpu.make_async_remote_copy(
            src_ref=part,
            dst_ref=part,
            send_sem=b_send.at[slot],
            recv_sem=b_recv.at[slot],
            device_id=device,
            device_id_type=MESH,
        ).start()

    def b_wait(dz, piece, other=False, count=1):
        if other:
            slot = {0: 12, -1: 13, 1: 17, 2: 21}[dz] + piece
        else:
            slot = {-1: 0, 1: 4, 2: 8}[dz] + piece
        part = b_piece(dz, 1 - core if other else core, piece, count)
        pltpu.make_async_copy(part, part, b_recv.at[slot]).wait()

    def b_relay(dz, piece):
        b_wait(dz, piece)
        b_go(dz, piece, -dz)
        b_go(dz, piece, 0)

    def b_rest(dz):
        for piece in {0: (), -1: (2, 3), 1: (1, 0), 2: (0, 3, 1, 2)}[dz]:
            b_wait(dz, piece)
            b_go(dz, piece, 0)
        if dz == 0:
            b_wait(0, 0, True, 4)
        else:
            for piece in range(4):
                b_wait(dz, piece, True)

    def depth(dx):
        return pl.ds(pl.multiple_of(wrap(x + dx) * 512, 512), 512)

    def add(half, blocks):
        rows = pl.ds(half * 512, 512)
        width = 512 if blocks[0][1] is None else 1024

        def one(n, carry):
            cols = pl.ds(pl.multiple_of(n * width, width), width)
            part = None
            for dy, dx in blocks:
                group, k = wrap(y + dy), slice(None) if dx is None else depth(dx)
                term = jnp.dot(a_buf[group, rows, k], b_buf[group, k, cols], preferred_element_type=F32)
                part = term if part is None else part + term
            total[rows, cols] += part
            return carry

        lax.fori_loop(0, 1024 // width, one, 0)

    halves = (0, 1)
    steps = (1, -1)
    close = (0, -1, 1)
    for step in steps:
        for half in halves:
            a_go(half, 0, 0, 0, step, None)
    for step in steps:
        for half in halves:
            a_go(half, 0, 0, 1, step, None)
    load_b.wait()
    for i in range(8):
        rows = pl.ds(pl.multiple_of(core * 1024 + i * TILE, TILE), TILE)
        for j in range(8):
            keep = rm_ref[i, j].astype(F32)
            cols = slice(j * TILE, (j + 1) * TILE)
            block = b_stage[i * TILE : (i + 1) * TILE, cols].astype(F32) * keep
            b_buf[z, rows, cols] = block.astype(BF16)
    total[256:, :] = jnp.zeros((768, 1024), F32)
    pass_on(0)
    for piece in (0, 1):
        b_go(0, piece, 1)
        b_go(0, 3 - piece, -1)
    b_go(0, 0, 0, 4)

    for half in halves:
        a_wait(half, -1, 0)
        a_go(half, -1, 0, 0, 1, 0)
        a_wait(half, 1, 0)
        a_go(half, 1, 0, 0, -1, 1)
    for first in (-1, 1):
        for half in halves:
            for step in steps:
                a_go(half, first, 0, 1, step, None)
    for piece in (2, 3):
        b_go(0, piece, 1)
        b_go(0, 3 - piece, -1)
    pass_on(1)

    def arrived(first):
        for half in halves:
            a_wait(half, first, -1)
            a_wait(half, first, 1)

    def relay(first):
        for half in halves:
            a_go(half, first, -1, 1, 1, 0)
            a_go(half, first, 1, 1, -1, 1)

    def gone(first):
        for half in halves:
            for side in steps:
                a_sent.pop(a_slot(half, first, side, side)).wait_send()

    arrived(0)
    relay(0)
    pass_on(2)
    for half in halves:
        a_wait(half, 2, 0, -1)
        a_wait(half, 2, 0, 1)
        for step in steps:
            a_go(half, 2, 0, 1, step, None)
    pass_on(3)
    for piece in (0, 1):
        b_relay(-1, piece)
        b_relay(1, 3 - piece)
    pass_on(4)
    for dz in (0, 1, -1):
        b_rest(dz)
    pass_on(5)

    def in_time(half, dy, dx):
        pl.when(near != (2 - dy) % SIDE)(lambda: add(half, dx(dy)))

    def late(half, dy, dx):
        pl.when(near == (2 - dy) % SIDE)(lambda: add(half, dx(dy)))

    def whole_row(dy):
        return [(dy, None)]

    def three(dy):
        return [(dy, dx) for dx in close]

    in_time(0, 0, whole_row)
    gone(-1)
    arrived(-1)
    relay(-1)
    pass_on(6)
    a_end(1, 0)
    in_time(1, 0, whole_row)
    arrived(1)
    for half in halves:
        for dy in (-1, 1):
            in_time(half, dy, three)
    gone(2)
    relay(1)
    arrived(2)
    relay(2)
    b_rest(2)
    for half in halves:
        late(half, 0, whole_row)
        for dy in (-1, 1):
            late(half, dy, three)
    add(1, three(2))
    for first in close:
        a_end(0, first)
    add(0, three(2) + [(-1, 2), (1, 2)])
    a_end(1, -1)
    a_end(1, 1)
    add(1, [(-1, 2), (1, 2)])
    a_end(1, 2)
    a_end(0, 2)

    order = (0, 1, 3, 2)

    def strips_of(part):
        found = []
        for dz in range(SIDE):
            there_y = wrap(y + (part - dz) % SIDE)
            for there_core in range(2):
                found.append((wrap(z + dz) * 2 + there_core, there_y))
        return found

    def finish(part, side):
        cols = slice(side * 512, side * 512 + 512)
        strips = strips_of(part)
        rows = [pl.ds(pl.multiple_of(g * TILE + v * 32, 32), 32) for g, v in strips]
        group, k = wrap(y + 2), depth(2)

        value = jnp.concatenate([total[r, cols] for r in rows], axis=0)
        lhs = jnp.concatenate([a_buf[group, r, k] for r in rows], axis=0)
        value += jnp.dot(lhs, b_buf[group, k, cols], preferred_element_type=F32)
        for i, (g, v) in enumerate(strips):
            for j in range(4):
                keep = om_ref[g, side * 4 + j].astype(F32)
                block = value[i * 32 : (i + 1) * 32, j * TILE : (j + 1) * TILE] * keep
                kept[pl.ds(g * 16 + v * 4, 4), :, pl.ds((side * 4 + j) * TILE, TILE)] = block.reshape(
                    4, 8, TILE
                ).astype(BF16)

    def hand_out(part):
        def one(t, carry):
            dz = lax.rem(t, 4)
            to_row = wrap(z + dz) * 2 + lax.rem(core + t // 16, 2)
            to_y = lax.rem(y + part + 4 - dz, 4)
            to_col = to_y * 4 + lax.rem(x + t + t // 4, 4)
            pltpu.make_async_remote_copy(
                src_ref=kept.at[to_row * 16 + to_col],
                dst_ref=out_ref.at[me],
                send_sem=x_send,
                recv_sem=x_recv,
                device_id=(to_row, to_col),
                device_id_type=MESH,
            ).start()
            return carry

        lax.fori_loop(1 if part == 0 else 0, 32, one, 0)

    finish(order[0], 0)
    finish(order[0], 1)
    for now, later in zip(order, order[1:]):
        finish(later, 0)
        hand_out(now)
        finish(later, 1)
    hand_out(order[-1])
    own = pltpu.make_async_copy(kept.at[me], out_ref.at[me], own_sem)
    own.start()

    for copy in a_sent.values():
        copy.wait_send()
    for slot in range(25):
        part = b_piece(0, core, 0, 4 if slot == 12 else 1)
        pltpu.make_async_copy(part, part, b_send.at[slot]).wait()
    own.wait()
    pltpu.make_async_copy(kept.at[pl.ds(0, 127)], kept.at[pl.ds(0, 127)], x_send).wait()
    pltpu.make_async_copy(out_ref.at[pl.ds(0, 127)], out_ref.at[pl.ds(0, 127)], x_recv).wait()


def flatten_kernel(in_ref, out_ref):
    out_ref[...] = in_ref[...].reshape(out_ref.shape)


def local(left_amps, right_ints, left_mask, right_mask, result_mask):
    hbm = pl.BlockSpec(memory_space=pltpu.HBM)
    anywhere = pl.BlockSpec(memory_space=pl.ANY)
    strips = pl.pallas_call(
        contract,
        out_shape=jax.ShapeDtypeStruct((128, 8, 1024), BF16),
        in_specs=[hbm] * 5,
        out_specs=anywhere,
        scratch_shapes=[
            pltpu.VMEM((4, 1024, 2048), BF16),
            pltpu.VMEM((4, 2048, 1024), BF16),
            pltpu.VMEM((1024, 512), BF16),
            pltpu.VMEM((1024, 1024), BF16),
            pltpu.VMEM((1024, 1024), F32),
            pltpu.VMEM((128, 8, 1024), BF16),
            pltpu.SemaphoreType.DMA((5,)),
            pltpu.SemaphoreType.DMA((40,)),
            pltpu.SemaphoreType.DMA((40,)),
            pltpu.SemaphoreType.DMA((25,)),
            pltpu.SemaphoreType.DMA((25,)),
            pltpu.SemaphoreType.DMA(()),
            pltpu.SemaphoreType.DMA(()),
            pltpu.SemaphoreType.DMA(()),
            pltpu.SemaphoreType.REGULAR((6,)),
            pltpu.SMEM((4, 8), jnp.int32),
            pltpu.SMEM((8, 8), jnp.int32),
            pltpu.SMEM((8, 8), jnp.int32),
        ],
        compiler_params=pltpu.CompilerParams(
            collective_id=0, has_side_effects=True, vmem_limit_bytes=46 * MIB
        ),
        name="contract",
    )(
        *(
            pltpu.with_memory_space_constraint(array, pltpu.HBM)
            for array in (left_mask.T, right_mask, result_mask, left_amps, right_ints)
        )
    )
    return pl.pallas_call(
        flatten_kernel,
        grid=(2,),
        in_specs=[pl.BlockSpec((64, 8, 1024), lambda p: (p, 0, 0))],
        out_specs=pl.BlockSpec((64, 8192), lambda p: (p, 0)),
        out_shape=jax.ShapeDtypeStruct((128, 8192), BF16),
        compiler_params=pltpu.CompilerParams(vmem_limit_bytes=12 * MIB),
        name="flatten",
    )(strips)


def solution(mesh):
    in_specs = (P("row", "col"), P("row", "col"), P("row", "col"), P("row", "col"), P("row", "col"))
    out_specs = P(None, ("row", "col"))
    return jax.shard_map(local, mesh=mesh, in_specs=in_specs, out_specs=out_specs, check_vma=False)
```
